32 devices in a mesh: lon: 8 (over z, x), lat: 4 (over y, core).
Axes of the slice: x: 2, y: 2, z: 4, core: 2. Of those that a mesh axis runs over, the one named last changes fastest.
Arguments:
- control_fields: float32 [2, 4, 544, 1536], P(None, None, 'lon', 'lat'), may hold values from -4 to 4
- unexplained_elevation: float32 [544, 1536], P('lon', 'lat'), may hold values from -6 to 6
- diffusivity: float32 [544, 1536], P('lon', 'lat'), may hold values from 0.15 to 0.49
- depth_levels: int32 [544, 1536], P('lon', 'lat'), may hold values from 0 to 4
- fold_partner: int32 [544], replicated, may hold values from 0 to 543, as said below
- prior_sigmas: float32 [2, 4], replicated, may hold values from 0.5 to 2
- haline_thermal_ratio: float32 [544, 1536], P('lon', 'lat'), may hold values from -0.6 to 0.6
- expansion_coefficients: float32 [2, 4], replicated, may hold values from -3 to 3
Outputs:
- state_fields: float32 [2, 4, 544, 1536], P(None, None, 'lon', 'lat')
- sea_height: float32 [544, 1536], P('lon', 'lat')
The draws below stay inside these ranges and needn't reach their ends.
Inputs may be any that keep to these rules, and one draw needn't show every extreme that they name: `fold_partner`: column i's fold partner lies in the block of 68 columns with block index (8 - (i div 68)) mod (8); within one block the partners are distinct.
All inputs are finite; a program needn't handle non-finite values.
Results may differ from the reference program's by a relative error of at most 0.0003.
Values sent between devices are 32-bit elements; how exact they have to be, the bound alone decides.
A program may use at most 64 MiB of HBM per device.

```python
import math
import jax
import jax.numpy as jnp
from jax import lax

DEPTH_STRATA = 4
CLON = 68
PASSES = 4
NLON = 544
NLAT = 1536


def draw_control_fields(key, part):
    rough_part = jax.random.normal(key, (2, DEPTH_STRATA, NLON, NLAT), jnp.float32)
    return jnp.clip(rough_part, -4.0, 4.0)


def draw_fold_partner(key, part):
    blocks = NLON // CLON
    block_keys = jax.random.split(key, blocks)
    orders = jax.vmap(lambda one_key: jax.random.permutation(one_key, CLON))(block_keys)
    mirror = ((blocks - jnp.arange(blocks, dtype=jnp.int32)) % blocks)[:, None] * CLON
    return (mirror + orders.astype(jnp.int32)).reshape(NLON)


def place_ends(values, rng, low, top_value):
    spot = [jax.random.randint(jax.random.fold_in(rng, axis), (), 0, length) for axis, length in enumerate(values.shape)]
    main_axis = values.shape.index(max(values.shape))
    neighbour = spot[:main_axis] + [(spot[main_axis] + 1) % values.shape[main_axis]] + spot[main_axis + 1:]
    return values.at[tuple(spot)].set(low).at[tuple(neighbour)].set(top_value)


def levels(rng, extent, cuts, smallest, largest):
    loudness = 1.0
    for axis_at, blocks in cuts:
        heights = jax.random.uniform(jax.random.fold_in(jax.random.fold_in(rng, 6), axis_at), (blocks,), jnp.float32, smallest / len(cuts), largest / len(cuts))
        loudness = loudness * jnp.repeat(jnp.exp(heights), extent[axis_at] // blocks).reshape((-1,) + (1,) * (len(extent) - 1 - axis_at))
    return loudness


def centred(key, dims, deviation, limit, shards=(), kind=jnp.bfloat16):
    result = jax.random.normal(key, dims, jnp.float32) * deviation
    if len(shards) > 0:
        result = levels(key, dims, shards, -0.22, 0.18) * result
    return jnp.clip(result, min=-limit, max=limit).astype(kind)


def setup_inputs(seed: int = 0) -> dict:
    streams_of = jax.random.split(jax.random.key(seed), 9)
    control_fields = draw_control_fields(jax.random.fold_in(streams_of[8], 71), 0)
    unexplained_elevation = centred(streams_of[1], (NLON, NLAT), 1.0, 6.0, ((0, 8), (1, 4)), jnp.float32)
    diffusivity = jnp.clip(jnp.exp(math.log(0.49) - 1.1837701 * jax.random.uniform(streams_of[2], (NLON, NLAT), jnp.float32) ** levels(streams_of[2], (NLON, NLAT), ((0, 8), (1, 4)), -0.2, 0.2)), 0.15, 0.49)
    depth_levels = place_ends(jax.random.randint(streams_of[3], (NLON, NLAT), 0, DEPTH_STRATA + 1), jax.random.fold_in(streams_of[3], 1), 0, DEPTH_STRATA).astype(jnp.int32)
    fold_partner = draw_fold_partner(jax.random.fold_in(streams_of[8], 71), 0)
    prior_sigmas = jnp.clip(jnp.exp(jax.random.uniform(streams_of[5], (2, DEPTH_STRATA), jnp.float32, math.log(0.5), math.log(2.0))), 0.5, 2.0)
    haline_thermal_ratio = jnp.clip(jax.random.uniform(streams_of[6], (NLON, NLAT), jnp.float32, -0.6, 0.6) * levels(streams_of[6], (NLON, NLAT), ((0, 8), (1, 4)), -0.4, 0.0), -0.6, 0.6)
    expansion_coefficients = centred(streams_of[7], (2, DEPTH_STRATA), 0.3, 3.0, (), jnp.float32)
    return {"control_fields": control_fields, "unexplained_elevation": unexplained_elevation, "diffusivity": diffusivity, "depth_levels": depth_levels, "fold_partner": fold_partner, "prior_sigmas": prior_sigmas, "haline_thermal_ratio": haline_thermal_ratio, "expansion_coefficients": expansion_coefficients}


def reference(control_fields, unexplained_elevation, diffusivity, depth_levels, fold_partner, prior_sigmas, haline_thermal_ratio, expansion_coefficients):
    kappa_east = jnp.roll(diffusivity, -1, axis=0)
    kappa_north = jnp.concatenate([diffusivity[:, 1:], diffusivity[fold_partner, -1:]], axis=1)

    def lone_stratum(ocean_elevation, level_index):
        wet_cells = (level_index < depth_levels).astype(jnp.float32)
        wet_east = jnp.roll(wet_cells, -1, axis=0)
        wet_north = jnp.concatenate([wet_cells[:, 1:], wet_cells[fold_partner, -1:]], axis=1)
        east_face = diffusivity * kappa_east * wet_cells * wet_east
        west_face = jnp.roll(east_face, 1, axis=0)
        north_face = diffusivity * kappa_north * wet_cells * wet_north
        south_face = jnp.concatenate([jnp.zeros_like(north_face[:, :1]), north_face[:, :-1]], axis=1)
        stratum_entries = lax.dynamic_index_in_dim(control_fields, level_index, 1, keepdims=False) * wet_cells
        for repeat in range(PASSES):
            east_value = jnp.roll(stratum_entries, -1, axis=1)
            west_value = jnp.roll(stratum_entries, 1, axis=1)
            north_value = jnp.concatenate([stratum_entries[:, :, 1:], stratum_entries[:, fold_partner, -1:]], axis=2)
            south_value = jnp.concatenate([jnp.zeros_like(stratum_entries[:, :, :1]), stratum_entries[:, :, :-1]], axis=2)
            stratum_entries = (stratum_entries + east_face * (east_value - stratum_entries)
                           + west_face * (west_value - stratum_entries)
                           + north_face * (north_value - stratum_entries)
                           + south_face * (south_value - stratum_entries))
        sigma_factor = lax.dynamic_index_in_dim(prior_sigmas, level_index, 1, keepdims=False)
        expansion_pair = lax.dynamic_index_in_dim(expansion_coefficients, level_index, 1, keepdims=False)
        thermal_grid = sigma_factor[0] * stratum_entries[0]
        saltiness_grid = sigma_factor[1] * stratum_entries[1] + haline_thermal_ratio * thermal_grid
        ocean_elevation = ocean_elevation + (expansion_pair[0] * thermal_grid + expansion_pair[1] * saltiness_grid)
        return ocean_elevation, (thermal_grid, saltiness_grid)

    ocean_elevation, (thermal_columns, saltiness_columns) = lax.scan(lone_stratum, unexplained_elevation, jnp.arange(DEPTH_STRATA, dtype=jnp.int32))
    return jnp.stack([thermal_columns, saltiness_columns]), ocean_elevation
```

```python
import functools

import jax
import jax.numpy as jnp
from jax import lax
from jax.experimental import pallas as pl
from jax.experimental.pallas import tpu as pltpu
from jax.sharding import PartitionSpec as P

PASSES = 4
LANES = 128
STRAIGHT_ROWS = (1, 2, 3, 2, 1)
MIRROR_ROWS = (2, 3, 4, 3, 2)
MESH = pl.DeviceIdType.MESH


def exchange_kernel(
    n_lon, n_lat,
    f_ref, k_ref, d_ref,
    ew_out, p_out, c_out, q_out,
    ew_buf, p_buf, pt_buf, q_buf, send_sem, recv_sem, local_sem,
):
    stacked, lon_cells, lat_cells = f_ref.shape
    b = lax.axis_index("lon")
    a_lat = lax.axis_index("lat")
    has_n = a_lat < n_lat - 1
    has_s = a_lat > 0
    is_top = a_lat == n_lat - 1
    east = lax.rem(b + 1, n_lon)
    west = lax.rem(b + n_lon - 1, n_lon)
    north = lax.rem(a_lat + 1, n_lat)
    south = lax.rem(a_lat + n_lat - 1, n_lat)

    straight = [
        (slot, STRAIGHT_ROWS[slot], lax.rem(b - (slot - 2) + n_lon, n_lon))
        for slot in (0, 1, 3, 4)
    ]
    mirrored = [
        (5 + slot, MIRROR_ROWS[slot], lax.rem((slot - 2) - b + 2 * n_lon, n_lon))
        for slot in range(5)
    ]

    barrier = pltpu.get_barrier_semaphore()

    def hail(lon, lat):
        pl.semaphore_signal(
            barrier, inc=1, device_id={"lon": lon, "lat": lat}, device_id_type=MESH
        )

    hail(east, a_lat)
    hail(west, a_lat)

    @pl.when(has_n)
    def _():
        for lon in (west, b, east):
            hail(lon, north)

    @pl.when(has_s)
    def _():
        for lon in (west, b, east):
            hail(lon, south)

    @pl.when(is_top)
    def _():
        for _, _, target in straight:
            hail(target, a_lat)
        for _, _, target in mirrored:
            @pl.when(target != b)
            def _():
                hail(target, a_lat)

    expected = 2 + jnp.where(has_n, 3, 0) + jnp.where(has_s, 3, 0) + jnp.where(is_top, 4, 0)
    for _, _, target in mirrored:
        expected = expected + jnp.where(jnp.logical_and(is_top, target != b), 1, 0)

    def read(a, rows, columns):
        if a < stacked:
            return f_ref[a, rows, columns]
        if a == stacked:
            return k_ref[rows, columns]
        return d_ref[rows, columns].astype(jnp.float32)

    arrays = stacked + 2
    everything = slice(0, lat_cells)
    for a in range(arrays):
        half = slice(4 * (a % 2), 4 * (a % 2) + 4)
        ew_buf[0, a // 2, half, :] = read(a, slice(lon_cells - 4, lon_cells), everything)
        ew_buf[1, a // 2, half, :] = read(a, slice(0, 4), everything)

    aligned = (lon_cells // 8) * 8
    for side in range(2):
        p_buf[side, aligned : aligned + 8, :] = jnp.zeros((8, LANES), jnp.float32)
        columns = slice(lat_cells - LANES, lat_cells) if side == 0 else slice(0, LANES)
        for start, count in ((0, aligned), (lon_cells - 8, 8)):
            rows = slice(start, start + count)
            group = lax.broadcasted_iota(jnp.int32, (count, LANES), 1) // 4
            packed = jnp.zeros((count, LANES), jnp.float32)
            for a in range(arrays):
                shift = (4 * a + (4 if side == 0 else 0)) % LANES
                moved = read(a, rows, columns)
                if shift:
                    moved = pltpu.roll(moved, shift, 1)
                packed = jnp.where(group == a, moved, packed)
            p_buf[side, rows, :] = packed

    def remote(src, dst, index, lon, lat):
        return pltpu.make_async_remote_copy(
            src_ref=src, dst_ref=dst, send_sem=send_sem.at[index], recv_sem=recv_sem.at[index],
            device_id={"lon": lon, "lat": lat}, device_id_type=MESH,
        )

    along = [
        remote(ew_buf.at[0], ew_out.at[0], 0, east, a_lat),
        remote(ew_buf.at[1], ew_out.at[1], 1, west, a_lat),
    ]
    tail = pl.ds(aligned, 8)
    head = pl.ds(0, 8)
    up = [
        remote(p_buf.at[0], p_out.at[0], 2, b, north),
        remote(p_buf.at[0, tail], c_out.at[0], 4, east, north),
        remote(p_buf.at[0, head], c_out.at[1], 5, west, north),
    ]
    down = [
        remote(p_buf.at[1], p_out.at[1], 3, b, south),
        remote(p_buf.at[1, tail], c_out.at[2], 6, east, south),
        remote(p_buf.at[1, head], c_out.at[3], 7, west, south),
    ]

    pl.semaphore_wait(barrier, expected)

    for copy in along:
        copy.start()

    @pl.when(has_n)
    def _():
        for copy in up:
            copy.start()

    @pl.when(has_s)
    def _():
        for copy in down:
            copy.start()

    strip_straight = [
        remote(q_buf.at[pl.ds(0, rows + 1)], q_out.at[slot, pl.ds(0, rows + 1)], 8 + slot, target, a_lat)
        for slot, rows, target in straight
    ]
    strip_mirrored = [
        (
            target != b,
            remote(q_buf.at[pl.ds(0, rows + 1)], q_out.at[slot, pl.ds(0, rows + 1)], 8 + slot, target, a_lat),
            pltpu.make_async_copy(
                q_buf.at[pl.ds(0, rows + 1)], q_out.at[slot, pl.ds(0, rows + 1)], local_sem.at[slot]
            ),
        )
        for slot, rows, target in mirrored
    ]
    own = pltpu.make_async_copy(q_buf, q_out.at[2], local_sem.at[2])

    @pl.when(is_top)
    def _():
        square = jnp.concatenate(
            [p_buf[0], jnp.zeros((LANES - p_buf.shape[1], LANES), jnp.float32)], axis=0
        )
        pt_buf[...] = square.T
        q_buf[0] = pt_buf[4 * stacked : 4 * stacked + 8, :]
        for r in range(4):
            q_buf[1 + r] = pt_buf[pl.ds(3 - r, stacked, stride=4), :]
        for copy in strip_straight:
            copy.start()
        for away, copy, stay in strip_mirrored:
            @pl.when(away)
            def _():
                copy.start()

            @pl.when(jnp.logical_not(away))
            def _():
                stay.start()
        own.start()

    for copy in along:
        copy.wait_send()
        copy.wait_recv()

    @pl.when(has_n)
    def _():
        for copy in up:
            copy.wait_send()
        for copy in down:
            copy.wait_recv()

    @pl.when(has_s)
    def _():
        for copy in down:
            copy.wait_send()
        for copy in up:
            copy.wait_recv()

    @pl.when(is_top)
    def _():
        for copy in strip_straight:
            copy.wait_send()
            copy.wait_recv()
        for away, copy, stay in strip_mirrored:
            @pl.when(away)
            def _():
                copy.wait_send()
                copy.wait_recv()

            @pl.when(jnp.logical_not(away))
            def _():
                stay.wait()
        own.wait()


def fold_strip(n_lon, lon_cells, b, q_ref, fp_ref, ghost_ref):
    lane = lax.broadcasted_iota(jnp.int32, (8, LANES), 1)
    sublane = lax.broadcasted_iota(jnp.int32, (8, LANES), 0)
    level = (sublane % 4).astype(jnp.float32)

    def spread(row):
        return jnp.broadcast_to(row, (8, LANES))

    def take(values, index):
        return jnp.take_along_axis(values, index, axis=1, mode="promise_in_bounds")

    kinds = {"S": STRAIGHT_ROWS, "M": MIRROR_ROWS}
    field, kappa, depth, index = {}, {}, {}, {}
    for kind, rows in kinds.items():
        for o in range(-2, 3):
            slot = o + 2 + (0 if kind == "S" else 5)
            block = lax.rem((b if kind == "S" else -b) + o + 2 * n_lon, n_lon)
            index[kind, o] = spread(fp_ref[pl.ds(block, 1), :])
            for r in range(rows[o + 2]):
                kappa[kind, o, r] = spread(q_ref[slot, 0, 3 - r : 4 - r, :])
                depth[kind, o, r] = spread(q_ref[slot, 0, 7 - r : 8 - r, :])
                values = q_ref[slot, 1 + r]
                field[kind, o, r] = jnp.where(depth[kind, o, r] > level, values, 0.0)

    other = {"S": "M", "M": "S"}

    def sides(table, kind, o, r):
        here = table[kind, o, r]
        from_east = table.get((kind, o + 1, r), here)
        from_west = table.get((kind, o - 1, r), here)
        towards = jnp.where(
            lane == lon_cells - 1, pltpu.roll(from_east, lon_cells - 1, 1), pltpu.roll(here, LANES - 1, 1)
        )
        back = jnp.where(
            lane == 0, pltpu.roll(from_west, LANES - lon_cells + 1, 1), pltpu.roll(here, 1, 1)
        )
        return towards, back

    def above(table, kind, o, r):
        if r:
            return table[kind, o, r - 1]
        return take(table[other[kind], -o, 0], index[kind, o])

    faces = {}
    ghosts = []

    def ghost_row(table):
        own = take(table["M", 0, 0], index["S", 0])
        right = take(table["M", -1, 0], index["S", 1])
        left = take(table["M", 1, 0], index["S", -1])
        result = jnp.where(
            lane < 16,
            pltpu.roll(left, (16 - lon_cells) % LANES, 1),
            jnp.where(
                lane < 16 + lon_cells, pltpu.roll(own, 16, 1), pltpu.roll(right, 16 + lon_cells, 1)
            ),
        )
        return jnp.where(jnp.logical_and(lane >= 12, lane < 20 + lon_cells), result, 0.0)

    ghost_kappa = ghost_row(kappa)
    ghost_depth = ghost_row(depth)
    ghosts.append(ghost_row(field))
    for step in range(1, PASSES):
        renewed = {}
        for kind, rows in kinds.items():
            for o in range(-2, 3):
                for r in range(rows[o + 2] - step):
                    if (kind, o, r) not in faces:
                        ke, kw = sides(kappa, kind, o, r)
                        de, dw = sides(depth, kind, o, r)
                        kn, dn = above(kappa, kind, o, r), above(depth, kind, o, r)
                        ks, ds = kappa[kind, o, r + 1], depth[kind, o, r + 1]
                        k0, d0 = kappa[kind, o, r], depth[kind, o, r]
                        faces[kind, o, r] = [
                            jnp.where(jnp.minimum(d0, d) > level, k0 * k, 0.0)
                            for k, d in ((ke, de), (kw, dw), (kn, dn), (ks, ds))
                        ]
                    fe, fw, fn, fs = faces[kind, o, r]
                    x = field[kind, o, r]
                    xe, xw = sides(field, kind, o, r)
                    xn = above(field, kind, o, r)
                    xs = field[kind, o, r + 1]
                    renewed[kind, o, r] = (
                        x + fe * (xe - x) + fw * (xw - x) + fn * (xn - x) + fs * (xs - x)
                    )
        field.update(renewed)
        ghosts.append(ghost_row(field))
    meta = jnp.where(sublane == 0, ghost_kappa, ghost_depth)
    stack = jnp.concatenate(
        ghosts + [meta, jnp.zeros((LANES - 8 * (PASSES + 1), LANES), jnp.float32)], axis=0
    )
    ghost_ref[...] = stack.T


def compute_kernel(
    n_lon, n_lat,
    f_ref, elev_ref, k_ref, d_ref, ratio_ref, fp_ref, sigma_ref, expand_ref,
    ew_ref, p_ref, c_ref, q_ref,
    state_ref, height_ref,
    xa, xb, kx, dx, faces, px, ghost_ref,
):
    stacked, lon_cells, lat_cells = f_ref.shape
    levels = stacked // 2
    b = lax.axis_index("lon")
    a_lat = lax.axis_index("lat")
    is_top = a_lat == n_lat - 1
    is_bottom = a_lat == 0
    rows_total = xa.shape[1]
    tiles = rows_total // 8
    wide = xa.shape[2]
    end = 16 + lon_cells

    @pl.when(is_top)
    def _():
        fold_strip(n_lon, lon_cells, b, q_ref, fp_ref, ghost_ref)

    zero_tile = jnp.zeros((8, wide), jnp.float32)
    for ref in (xa, xb):
        for f in range(stacked):
            ref[f, 0:8, :] = zero_tile
            ref[f, rows_total - 8 : rows_total, :] = zero_tile
    for ref in (kx, dx):
        ref[0:16, :] = jnp.zeros((16, wide), jnp.float32)
        ref[rows_total - 8 : rows_total, :] = zero_tile
    for f in range(stacked):
        xa[f, 8:16, :] = zero_tile
    px[...] = jnp.zeros(px.shape, jnp.float32)

    @pl.when(jnp.logical_not(is_bottom))
    def _():
        px[0, 16:end, :] = p_ref[0, 0:lon_cells, :]
        px[0, 12:16, :] = c_ref[0, lon_cells % 8 - 4 : lon_cells % 8, :]
        px[0, end : end + 4, :] = c_ref[1, 0:4, :]

    @pl.when(jnp.logical_not(is_top))
    def _():
        px[1, 16:end, :] = p_ref[1, 0:lon_cells, :]
        px[1, 12:16, :] = c_ref[2, lon_cells % 8 - 4 : lon_cells % 8, :]
        px[1, end : end + 4, :] = c_ref[3, 0:4, :]

    lane = lax.broadcasted_iota(jnp.int32, (rows_total, LANES), 1)

    def place(ref, own, a):
        ref[16:end, 0:lat_cells] = own
        half = slice(4 * (a % 2), 4 * (a % 2) + 4)
        ref[12:16, 0:lat_cells] = ew_ref[0, a // 2, half, :]
        ref[end : end + 4, 0:lat_cells] = ew_ref[1, a // 2, half, :]
        below = pltpu.roll(px[0], LANES - 4 - 4 * a, 1)
        up = px[1]
        if a:
            up = pltpu.roll(up, LANES - 4 * a, 1)
        ref[:, lat_cells:wide] = jnp.where(lane < 4, up, jnp.where(lane >= LANES - 4, below, 0.0))

    for f in range(stacked):
        place(xa.at[f], f_ref[f], f)
    place(kx, k_ref[...], stacked)
    place(dx, d_ref[...].astype(jnp.float32), stacked + 1)

    def refresh(ref, which):
        moved = ghost_ref[0:rows_total, :]
        if which:
            moved = pltpu.roll(moved, LANES - which, 1)
        ref[:, lat_cells:wide] = jnp.where(lane == 0, moved, ref[:, lat_cells:wide])

    @pl.when(is_top)
    def _():
        refresh(kx, 8 * PASSES)
        refresh(dx, 8 * PASSES + 1)

    for i in range(1, tiles - 1):
        at = slice(8 * i, 8 * i + 8)
        k0, d0 = kx[at, :], dx[at, :]
        pairs = []
        for rows in (slice(8 * i + 1, 8 * i + 9), slice(8 * i - 1, 8 * i + 7)):
            pairs.append((kx[rows, :], dx[rows, :]))
        for shift in (wide - 1, 1):
            pairs.append((pltpu.roll(k0, shift, 1), pltpu.roll(d0, shift, 1)))
        pairs = [(k0 * k, jnp.minimum(d0, d)) for k, d in pairs]
        for level in range(levels):
            total = jnp.ones((8, wide), jnp.float32)
            for side, (product, least) in enumerate(pairs):
                face = jnp.where(least > float(level), product, 0.0)
                faces[level, side, at, :] = face
                total = total - face
            faces[level, 4, at, :] = total
            for c in range(2):
                f = c * levels + level
                xa[f, at, :] = jnp.where(d0 > float(level), xa[f, at, :], 0.0)

    source, target = xa, xb
    for step in range(PASSES):
        @pl.when(is_top)
        def _(source=source, step=step):
            for f in range(stacked):
                refresh(source.at[f], 8 * step + f)

        def one_level(level, carry, source=source, target=target):
            for i in range(1, tiles - 1):
                at = slice(8 * i, 8 * i + 8)
                fe, fw, fn, fs, fc = [faces[level, side, at, :] for side in range(5)]
                for c in range(2):
                    f = c * levels + level
                    x = source[f, at, :]
                    xe = source[f, 8 * i + 1 : 8 * i + 9, :]
                    xw = source[f, 8 * i - 1 : 8 * i + 7, :]
                    xn = pltpu.roll(x, wide - 1, 1)
                    xs = pltpu.roll(x, 1, 1)
                    target[f, at, :] = fc * x + fe * xe + fw * xw + fn * xn + fs * xs
            return carry

        lax.fori_loop(0, levels, one_level, 0)
        source, target = target, source

    for start in range(0, lon_cells, 8):
        count = min(8, lon_cells - start)
        out = slice(start, start + count)
        at = slice(16 + start, 16 + start + count)
        ratio = ratio_ref[out, :]
        height = elev_ref[out, :]
        for level in range(levels):
            thermal = sigma_ref[0, level] * source[level, at, 0:lat_cells]
            salt = sigma_ref[1, level] * source[levels + level, at, 0:lat_cells] + ratio * thermal
            state_ref[level, out, :] = thermal
            state_ref[levels + level, out, :] = salt
            height = height + (expand_ref[0, level] * thermal + expand_ref[1, level] * salt)
        height_ref[out, :] = height


def local(
    n_lon, n_lat,
    control_fields,
    unexplained_elevation,
    diffusivity,
    depth_levels,
    fold_partner,
    prior_sigmas,
    haline_thermal_ratio,
    expansion_coefficients,
):
    levels, lon_cells, lat_cells = control_fields.shape[1:]
    stacked = 2 * levels
    fields = control_fields.reshape(stacked, lon_cells, lat_cells)
    partners = jnp.pad(
        (fold_partner % lon_cells).reshape(n_lon, lon_cells), ((0, 0), (0, LANES - lon_cells))
    )
    pairs = (stacked + 2) // 2
    tall = -(-lon_cells // 8) * 8
    f32 = jnp.float32
    vmem = pl.BlockSpec(memory_space=pltpu.VMEM)
    smem = pl.BlockSpec(memory_space=pltpu.SMEM)
    anywhere = pl.BlockSpec(memory_space=pl.ANY)
    halos = pl.pallas_call(
        functools.partial(exchange_kernel, n_lon, n_lat),
        name="exchange",
        out_shape=(
            jax.ShapeDtypeStruct((2, pairs, 8, lat_cells), f32),
            jax.ShapeDtypeStruct((2, tall, LANES), f32),
            jax.ShapeDtypeStruct((4, 8, LANES), f32),
            jax.ShapeDtypeStruct((10, 5, 8, LANES), f32),
        ),
        in_specs=[vmem] * 3,
        out_specs=(anywhere,) * 4,
        scratch_shapes=[
            pltpu.VMEM((2, pairs, 8, lat_cells), f32),
            pltpu.VMEM((2, tall, LANES), f32),
            pltpu.VMEM((LANES, LANES), f32),
            pltpu.VMEM((5, 8, LANES), f32),
            pltpu.SemaphoreType.DMA((18,)),
            pltpu.SemaphoreType.DMA((18,)),
            pltpu.SemaphoreType.DMA((10,)),
        ],
        compiler_params=pltpu.CompilerParams(collective_id=0, has_side_effects=True),
    )(fields, diffusivity, depth_levels)
    wide = lat_cells + LANES
    tiles = 16 + tall + 8
    state, height = pl.pallas_call(
        functools.partial(compute_kernel, n_lon, n_lat),
        name="diffuse",
        out_shape=(
            jax.ShapeDtypeStruct((stacked, lon_cells, lat_cells), f32),
            jax.ShapeDtypeStruct((lon_cells, lat_cells), f32),
        ),
        in_specs=[vmem] * 6 + [smem] * 2 + [vmem] * 4,
        out_specs=(vmem, vmem),
        scratch_shapes=[
            pltpu.VMEM((stacked, tiles, wide), f32),
            pltpu.VMEM((stacked, tiles, wide), f32),
            pltpu.VMEM((tiles, wide), f32),
            pltpu.VMEM((tiles, wide), f32),
            pltpu.VMEM((levels, 5, tiles, wide), f32),
            pltpu.VMEM((2, tiles, LANES), f32),
            pltpu.VMEM((LANES, LANES), f32),
        ],
        compiler_params=pltpu.CompilerParams(vmem_limit_bytes=40 * 1024 * 1024),
    )(
        fields, unexplained_elevation, diffusivity, depth_levels, haline_thermal_ratio,
        partners, prior_sigmas, expansion_coefficients, *halos,
    )
    return state.reshape(2, levels, lon_cells, lat_cells), height


def solution(mesh):
    return jax.shard_map(
        functools.partial(local, mesh.shape["lon"], mesh.shape["lat"]),
        mesh=mesh,
        in_specs=(
            P(None, None, "lon", "lat"),
            P("lon", "lat"),
            P("lon", "lat"),
            P("lon", "lat"),
            P(),
            P(),
            P("lon", "lat"),
            P(),
        ),
        out_specs=(P(None, None, "lon", "lat"), P("lon", "lat")),
        check_vma=False,
    )
```

```python
import functools

import jax
import jax.numpy as jnp
from jax import lax
from jax.experimental import pallas as pl
from jax.experimental.pallas import tpu as pltpu
from jax.sharding import PartitionSpec as P

PASSES = 4
LANES = 128
STRAIGHT_ROWS = (1, 2, 3, 2, 1)
MIRROR_ROWS = (2, 3, 4, 3, 2)
PLACES = (1, 0, 3)
MESH = pl.DeviceIdType.MESH


def exchange_kernel(
    n_lon, n_lat,
    f_ref, k_ref, d_ref,
    ew_out, kd_out, p_out, c_out, q_out,
    edge_buf, tail_buf, kd_buf, p_buf, send_sem, recv_sem, local_sem, load_sem,
):
    lon_cells, lat_cells = k_ref.shape
    b = lax.axis_index("lon")
    a_lat = lax.axis_index("lat")
    has_n = a_lat < n_lat - 1
    has_s = a_lat > 0
    is_top = a_lat == n_lat - 1
    east = lax.rem(b + 1, n_lon)
    west = lax.rem(b + n_lon - 1, n_lon)
    north = lax.rem(a_lat + 1, n_lat)
    south = lax.rem(a_lat + n_lat - 1, n_lat)

    loads = [
        pltpu.make_async_copy(
            f_ref.at[c, :, :, pl.ds(start, LANES)],
            edge_buf.at[side, :, pl.ds(4 * c, 4), :],
            load_sem.at[2 * side + c],
        )
        for side, start in ((0, lat_cells - LANES), (1, 0))
        for c in range(2)
    ]
    for copy in loads:
        copy.start()

    straight = [
        (slot, lax.rem(b - (slot - 2) + n_lon, n_lon))
        for slot in (0, 1, 3, 4)
    ]
    mirrored = [
        (5 + slot, lax.rem((slot - 2) - b + 2 * n_lon, n_lon))
        for slot in range(5)
    ]

    barrier = pltpu.get_barrier_semaphore()

    def hail(lon, lat):
        pl.semaphore_signal(
            barrier, inc=1, device_id={"lon": lon, "lat": lat}, device_id_type=MESH
        )

    hail(east, a_lat)
    hail(west, a_lat)

    @pl.when(has_n)
    def _():
        for lon in (west, b, east):
            hail(lon, north)

    @pl.when(has_s)
    def _():
        for lon in (west, b, east):
            hail(lon, south)

    @pl.when(is_top)
    def _():
        for _, target in straight:
            hail(target, a_lat)
        for _, target in mirrored:
            @pl.when(target != b)
            def _():
                hail(target, a_lat)

    expected = 2 + jnp.where(has_n, 3, 0) + jnp.where(has_s, 3, 0) + jnp.where(is_top, 4, 0)
    for _, target in mirrored:
        expected = expected + jnp.where(jnp.logical_and(is_top, target != b), 1, 0)

    def remote(src, dst, index, lon, lat):
        return pltpu.make_async_remote_copy(
            src_ref=src, dst_ref=dst, send_sem=send_sem.at[index], recv_sem=recv_sem.at[index],
            device_id={"lon": lon, "lat": lat}, device_id_type=MESH,
        )

    last = pl.ds(lon_cells - 4, 4)
    first = pl.ds(0, 4)
    far = [
        remote(f_ref.at[:, last], ew_out.at[0], 0, east, a_lat),
        remote(f_ref.at[:, first], ew_out.at[1], 1, west, a_lat),
    ]
    pl.semaphore_wait(barrier, expected)
    for copy in far:
        copy.start()

    for source, start in ((k_ref, 0), (d_ref, 4)):
        kd_buf[0, start : start + 4, :] = source[lon_cells - 4 : lon_cells, :].astype(jnp.float32)
        kd_buf[1, start : start + 4, :] = source[0:4, :].astype(jnp.float32)

    lane = lax.broadcasted_iota(jnp.int32, (8, LANES), 1)
    aligned = (lon_cells // 8) * 8
    for side in range(2):
        columns = slice(lat_cells - LANES, lat_cells) if side == 0 else slice(0, LANES)
        offset = 4 if side == 0 else 0
        packed = jnp.zeros((8, LANES), jnp.float32)
        for which, source in enumerate((k_ref, d_ref)):
            tail_buf[...] = jnp.zeros((8, LANES), jnp.float32)
            tail_buf[0 : lon_cells - aligned, :] = source[aligned:lon_cells, columns].astype(jnp.float32)
            for j in range(-(-lon_cells // 8)):
                if 8 * j < aligned:
                    moved = source[8 * j : 8 * j + 8, columns].astype(jnp.float32)
                else:
                    moved = tail_buf[...]
                shift = (8 * j + 4 * which + offset) % LANES
                if shift:
                    moved = pltpu.roll(moved, shift, 1)
                packed = jnp.where(lane // 4 == 2 * j + which, moved, packed)
        p_buf[side, :, 2 * LANES : 3 * LANES] = packed

    for copy in loads:
        copy.wait()
    for side in range(2):
        offset = 4 if side == 0 else 0
        for group in range(3):
            packed = jnp.zeros((8, LANES), jnp.float32)
            for col in range(32 * group, min(32 * group + 32, lon_cells)):
                shift = (4 * (col % 32) + offset) % LANES
                moved = edge_buf[side, col]
                if shift:
                    moved = pltpu.roll(moved, shift, 1)
                packed = jnp.where(lane // 4 == col % 32, moved, packed)
            place = PLACES[group] * LANES
            p_buf[side, :, place : place + LANES] = packed

    along = [
        remote(kd_buf.at[0], kd_out.at[0], 18, east, a_lat),
        remote(kd_buf.at[1], kd_out.at[1], 19, west, a_lat),
    ]
    tail = pl.ds(2 * LANES, 2 * LANES)
    head = pl.ds(LANES, 2 * LANES)
    up = [
        remote(p_buf.at[0], p_out.at[0], 2, b, north),
        remote(p_buf.at[0, :, tail], c_out.at[0], 4, east, north),
        remote(p_buf.at[0, :, head], c_out.at[1], 5, west, north),
    ]
    down = [
        remote(p_buf.at[1], p_out.at[1], 3, b, south),
        remote(p_buf.at[1, :, tail], c_out.at[2], 6, east, south),
        remote(p_buf.at[1, :, head], c_out.at[3], 7, west, south),
    ]

    for copy in along:
        copy.start()

    @pl.when(has_n)
    def _():
        for copy in up:
            copy.start()

    @pl.when(has_s)
    def _():
        for copy in down:
            copy.start()

    strip_straight = [
        remote(p_buf.at[0], q_out.at[slot], 8 + slot, target, a_lat) for slot, target in straight
    ]
    strip_mirrored = [
        (
            target != b,
            remote(p_buf.at[0], q_out.at[slot], 8 + slot, target, a_lat),
            pltpu.make_async_copy(p_buf.at[0], q_out.at[slot], local_sem.at[slot]),
        )
        for slot, target in mirrored
    ]
    own = pltpu.make_async_copy(p_buf.at[0], q_out.at[2], local_sem.at[2])

    @pl.when(is_top)
    def _():
        for copy in strip_straight:
            copy.start()
        for away, copy, stay in strip_mirrored:
            @pl.when(away)
            def _():
                copy.start()

            @pl.when(jnp.logical_not(away))
            def _():
                stay.start()
        own.start()

    for copy in far + along:
        copy.wait_send()
        copy.wait_recv()

    @pl.when(has_n)
    def _():
        for copy in up:
            copy.wait_send()
        for copy in down:
            copy.wait_recv()

    @pl.when(has_s)
    def _():
        for copy in down:
            copy.wait_send()
        for copy in up:
            copy.wait_recv()

    @pl.when(is_top)
    def _():
        for copy in strip_straight:
            copy.wait_send()
            copy.wait_recv()
        for away, copy, stay in strip_mirrored:
            @pl.when(away)
            def _():
                copy.wait_send()
                copy.wait_recv()

            @pl.when(jnp.logical_not(away))
            def _():
                stay.wait()
        own.wait()


def fold_strip(n_lon, lon_cells, b, q_ref, fp_ref, ghost_ref, coast_ref):
    lane = lax.broadcasted_iota(jnp.int32, (8, LANES), 1)
    sublane = lax.broadcasted_iota(jnp.int32, (8, LANES), 0)
    level = (sublane % 4).astype(jnp.float32)

    def spread(row):
        return jnp.broadcast_to(row, (8, LANES))

    def take(values, index):
        return jnp.take_along_axis(values, index, axis=1, mode="promise_in_bounds")

    kinds = {"S": STRAIGHT_ROWS, "M": MIRROR_ROWS}
    field, kappa, depth, index = {}, {}, {}, {}

    def tile(slot, place):
        return q_ref[slot, :, place * LANES : (place + 1) * LANES]

    def column_of(values, start):
        picked = take(values, 8 * (lane // 8) + start)
        return spread(jnp.sum(jnp.where(sublane == lane % 8, picked, 0.0), axis=0, keepdims=True))

    for kind, rows in kinds.items():
        for o in range(-2, 3):
            slot = o + 2 + (0 if kind == "S" else 5)
            block = lax.rem((b if kind == "S" else -b) + o + 2 * n_lon, n_lon)
            opposite = lax.rem(n_lon - block, n_lon)
            index[kind, o] = jnp.maximum(
                spread(fp_ref[pl.ds(block, 1), :]) - opposite * lon_cells, 0
            )
            parts = [tile(slot, place) for place in PLACES]
            meta = tile(slot, 2)
            for r in range(rows[o + 2]):
                kappa[kind, o, r] = column_of(meta, 3 - r)
                depth[kind, o, r] = column_of(meta, 7 - r)
                pieces = [take(part, 4 * (lane % 32) + 3 - r) for part in parts]
                values = jnp.where(
                    lane < 32, pieces[0], jnp.where(lane < 64, pieces[1], pieces[2])
                )
                field[kind, o, r] = jnp.where(depth[kind, o, r] > level, values, 0.0)

    other = {"S": "M", "M": "S"}

    def sides(table, kind, o, r):
        here = table[kind, o, r]
        from_east = table.get((kind, o + 1, r), here)
        from_west = table.get((kind, o - 1, r), here)
        towards = jnp.where(
            lane == lon_cells - 1, pltpu.roll(from_east, lon_cells - 1, 1), pltpu.roll(here, LANES - 1, 1)
        )
        back = jnp.where(
            lane == 0, pltpu.roll(from_west, LANES - lon_cells + 1, 1), pltpu.roll(here, 1, 1)
        )
        return towards, back

    def above(table, kind, o, r):
        if r:
            return table[kind, o, r - 1]
        return take(table[other[kind], -o, 0], index[kind, o])

    faces = {}
    ghosts = []

    def ghost_row(table):
        own = take(table["M", 0, 0], index["S", 0])
        right = take(table["M", -1, 0], index["S", 1])
        left = take(table["M", 1, 0], index["S", -1])
        result = jnp.where(
            lane < 4,
            pltpu.roll(left, (4 - lon_cells) % LANES, 1),
            jnp.where(
                lane < 4 + lon_cells, pltpu.roll(own, 4, 1), pltpu.roll(right, 4 + lon_cells, 1)
            ),
        )
        return jnp.where(lane < 8 + lon_cells, result, 0.0)

    ghost_kappa = ghost_row(kappa)
    ghost_depth = ghost_row(depth)
    ghosts.append(ghost_row(field))
    for step in range(1, PASSES):
        renewed = {}
        for kind, rows in kinds.items():
            for o in range(-2, 3):
                for r in range(rows[o + 2] - step):
                    if (kind, o, r) not in faces:
                        ke, kw = sides(kappa, kind, o, r)
                        de, dw = sides(depth, kind, o, r)
                        kn, dn = above(kappa, kind, o, r), above(depth, kind, o, r)
                        ks, ds = kappa[kind, o, r + 1], depth[kind, o, r + 1]
                        k0, d0 = kappa[kind, o, r], depth[kind, o, r]
                        faces[kind, o, r] = [
                            jnp.where(jnp.minimum(d0, d) > level, k0 * k, 0.0)
                            for k, d in ((ke, de), (kw, dw), (kn, dn), (ks, ds))
                        ]
                    fe, fw, fn, fs = faces[kind, o, r]
                    x = field[kind, o, r]
                    xe, xw = sides(field, kind, o, r)
                    xn = above(field, kind, o, r)
                    xs = field[kind, o, r + 1]
                    renewed[kind, o, r] = (
                        x + fe * (xe - x) + fw * (xw - x) + fn * (xn - x) + fs * (xs - x)
                    )
        field.update(renewed)
        ghosts.append(ghost_row(field))
    for step in range(PASSES):
        ghost_ref[step] = ghosts[step]
    for which, row in ((0, ghost_kappa), (1, ghost_depth)):
        square = jnp.concatenate([row, jnp.zeros((LANES - 8, LANES), jnp.float32)], axis=0).T
        coast_ref[which, 0:4, :] = jnp.zeros((4, LANES), jnp.float32)
        coast_ref[which, 4 : 8 + LANES - 4, :] = square[0:LANES, :]


def compute_kernel(
    n_lon, n_lat,
    f_ref, elev_ref, k_ref, d_ref, ratio_ref, fp_ref, sigma_ref, expand_ref,
    ew_hbm, kd_hbm, p_hbm, c_hbm, q_hbm,
    state_hbm, height_ref,
    xa, xb, ya, kx, dx, lon_k, lon_d, lat_k, lat_d, e_face, n_face,
    kd_ref, p_ref, c_ref, q_ref, ghost_ref, coast_ref, sems, out_sems,
):
    lon_cells, lat_cells = k_ref.shape
    wide = xa.shape[2]
    count = lon_cells + 8
    tall = kx.shape[0]
    b = lax.axis_index("lon")
    a_lat = lax.axis_index("lat")
    is_top = a_lat == n_lat - 1
    is_bottom = a_lat == 0

    small = [
        pltpu.make_async_copy(kd_hbm, kd_ref, sems.at[0]),
        pltpu.make_async_copy(p_hbm, p_ref, sems.at[1]),
        pltpu.make_async_copy(c_hbm, c_ref, sems.at[2]),
        pltpu.make_async_copy(q_hbm, q_ref, sems.at[3]),
    ]
    large = []
    for c in range(2):
        half = pl.ds(4 * c, 4)
        own = pl.ds(0, lat_cells)
        large += [
            pltpu.make_async_copy(ew_hbm.at[0, c], xa.at[pl.ds(0, 4), half, own], sems.at[4 + c]),
            pltpu.make_async_copy(
                ew_hbm.at[1, c], xa.at[pl.ds(lon_cells + 4, 4), half, own], sems.at[6 + c]
            ),
            pltpu.make_async_copy(f_ref.at[c], xa.at[pl.ds(4, lon_cells), half, own], sems.at[8 + c]),
        ]
    for copy in small + large:
        copy.start()

    sublane = lax.broadcasted_iota(jnp.int32, (8, LANES), 0)
    lane = lax.broadcasted_iota(jnp.int32, (8, LANES), 1)
    for ref, source in ((kx, k_ref), (dx, d_ref)):
        ref[0:8, :] = jnp.zeros((8, wide), jnp.float32)
        ref[8 : 8 + lon_cells, 0:lat_cells] = source[...].astype(jnp.float32)

    for copy in small:
        copy.wait()

    kx[4:8, 0:lat_cells] = kd_ref[0, 0:4, :]
    dx[4:8, 0:lat_cells] = kd_ref[0, 4:8, :]
    kx[8 + lon_cells : 12 + lon_cells, 0:lat_cells] = kd_ref[1, 0:4, :]
    dx[8 + lon_cells : 12 + lon_cells, 0:lat_cells] = kd_ref[1, 4:8, :]

    def part(ref, place):
        return ref[:, place * LANES : (place + 1) * LANES]

    def clean(present, values):
        return jnp.where(present, values, 0.0)

    no_n, no_s = jnp.logical_not(is_top), jnp.logical_not(is_bottom)
    south = [clean(no_s, part(p_ref.at[0], place)) for place in PLACES]
    north = [clean(no_n, part(p_ref.at[1], place)) for place in PLACES]
    south_west = clean(no_s, part(c_ref.at[0], 1))
    south_east = clean(no_s, part(c_ref.at[1], 0))
    north_west = clean(no_n, part(c_ref.at[2], 1))
    north_east = clean(no_n, part(c_ref.at[3], 0))

    def turned(values, shift):
        shift %= LANES
        return pltpu.roll(values, shift, 1) if shift else values

    def join(up, below, start):
        return jnp.where(
            lane < 4, turned(up, -start),
            jnp.where(lane >= LANES - 4, turned(below, LANES - 4 - start), 0.0),
        )

    for i in range(count):
        if i < 4:
            up, below, at = north_west, south_west, i
        elif i < 4 + lon_cells:
            col = i - 4
            up, below, at = north[col // 32], south[col // 32], col % 32
        else:
            up, below, at = north_east, south_east, i - 4 - lon_cells
        xa[i, :, lat_cells:wide] = join(up, below, 4 * at)

    south_k, north_k = clean(no_s, part(p_ref.at[0], 2)), clean(no_n, part(p_ref.at[1], 2))
    tail_col = (lon_cells // 8) * 8
    corners = (
        (pltpu.roll(clean(no_n, part(c_ref.at[2], 0)), 4, 0), pltpu.roll(clean(no_s, part(c_ref.at[0], 0)), 4, 0)),
        (pltpu.roll(clean(no_n, part(c_ref.at[3], 1)), 4, 0), pltpu.roll(clean(no_s, part(c_ref.at[1], 1)), 4, 0)),
    )
    for which, ref in enumerate((kx, dx)):
        from_west = join(corners[0][0], corners[0][1], tail_col + 4 * which)
        ref[0:8, lat_cells:wide] = jnp.where(sublane >= 4, from_west, 0.0)
        for j in range((tall - 8) // 8):
            piece = join(north_k, south_k, 8 * j + 4 * which)
            if 8 * j == tail_col:
                piece = jnp.where(sublane < 4, piece, join(corners[1][0], corners[1][1], 4 * which))
            ref[8 + 8 * j : 16 + 8 * j, lat_cells:wide] = piece

    @pl.when(is_top)
    def _():
        fold_strip(n_lon, lon_cells, b, q_ref, fp_ref, ghost_ref, coast_ref)
        for which, ref in enumerate((kx, dx)):
            for j in range(tall // 8):
                at = slice(8 * j, 8 * j + 8)
                ref[at, lat_cells:wide] = jnp.where(
                    lane == 0, coast_ref[which, at, :], ref[at, lat_cells:wide]
                )

    for j in range(tall // 8):
        at = slice(8 * j, 8 * j + 8)
        k0, d0 = kx[at, :], dx[at, :]
        lat_k[at, :] = k0 * pltpu.roll(k0, wide - 1, 1)
        lat_d[at, :] = jnp.minimum(d0, pltpu.roll(d0, wide - 1, 1))
        if j < tall // 8 - 1:
            after = slice(8 * j + 1, 8 * j + 9)
            lon_k[at, :] = k0 * kx[after, :]
            lon_d[at, :] = jnp.minimum(d0, dx[after, :])
        else:
            after = slice(8 * j + 1, 8 * j + 8)
            at = slice(8 * j, 8 * j + 7)
            lon_k[at, :] = kx[at, :] * kx[after, :]
            lon_d[at, :] = jnp.minimum(dx[at, :], dx[after, :])
            lon_k[tall - 1 : tall, :] = jnp.zeros((1, wide), jnp.float32)
            lon_d[tall - 1 : tall, :] = jnp.zeros((1, wide), jnp.float32)

    level = (lax.broadcasted_iota(jnp.int32, (8, wide), 0) % 4).astype(jnp.float32)

    def row(ref, i):
        return jnp.broadcast_to(ref[pl.ds(i + 4, 1), :], (8, ref.shape[1]))

    def make_faces(i, carry):
        e_face[i] = jnp.where(row(lon_d, i) > level, row(lon_k, i), 0.0)
        n_face[i] = jnp.where(row(lat_d, i) > level, row(lat_k, i), 0.0)
        return carry

    lax.fori_loop(0, count, make_faces, 0, unroll=4)

    for copy in large:
        copy.wait()

    def mask(i, carry):
        xa[i] = jnp.where(row(dx, i) > level, xa[i], 0.0)
        return carry

    lax.fori_loop(0, count, mask, 0, unroll=4)

    def advance(source, i, state):
        x, flux_west = state
        x_east = source[i + 1]
        flux_east = e_face[i] * (x_east - x)
        flux_north = n_face[i] * (pltpu.roll(x, wide - 1, 1) - x)
        fresh = ((x + flux_east) - flux_west) + (flux_north - pltpu.roll(flux_north, 1, 1))
        return fresh, (x_east, flux_east)

    def refresh(ref, step):
        @pl.when(is_top)
        def _():
            ghosts = ghost_ref[step]
            for i in range(step + 1, count - step - 1):
                ref[i, :, lat_cells:wide] = jnp.where(
                    lane == 0, turned(ghosts, -i), ref[i, :, lat_cells:wide]
                )

    def start_of(source, first):
        x = source[first]
        return x, e_face[first - 1] * (x - source[first - 1])

    source, target = xa, xb
    for step in range(PASSES - 1):
        refresh(source, step)
        first, stop = step + 1, count - step - 1

        def one(i, state, source=source, target=target):
            fresh, state = advance(source, i, state)
            target[i] = fresh
            return state

        lax.fori_loop(first, stop, one, start_of(source, first), unroll=2)
        source, target = target, source
    refresh(source, PASSES - 1)

    short = lax.broadcasted_iota(jnp.int32, (8, lat_cells), 0)
    sigma = jnp.zeros((8, lat_cells), jnp.float32)
    expand = jnp.zeros((8, lat_cells), jnp.float32)
    for c in range(2):
        for k in range(4):
            sigma = jnp.where(short == 4 * c + k, sigma_ref[c, k], sigma)
            expand = jnp.where(short == 4 * c + k, expand_ref[c, k], expand)

    def balance(i, state):
        fresh, state = advance(source, i, state)
        scaled = sigma * fresh[:, 0:lat_cells]
        col = i - 4
        ratio = jnp.broadcast_to(ratio_ref[pl.ds(col, 1), :], (8, lat_cells))
        result = scaled + jnp.where(short >= 4, ratio * pltpu.roll(scaled, 4, 0), 0.0)
        ya[col] = result
        height_ref[pl.ds(col, 1), :] = elev_ref[pl.ds(col, 1), :] + jnp.sum(
            expand * result, axis=0, keepdims=True
        )
        return state

    state = start_of(source, 4)
    middle = (lon_cells // 4) * 2
    bounds = (0, middle, lon_cells)
    outs = []
    for chunk in range(2):
        lo, hi = bounds[chunk], bounds[chunk + 1]
        state = lax.fori_loop(lo + 4, hi + 4, balance, state, unroll=2)
        for c in range(2):
            copy = pltpu.make_async_copy(
                ya.at[pl.ds(lo, hi - lo), pl.ds(4 * c, 4), :],
                state_hbm.at[c, pl.ds(lo, hi - lo)],
                out_sems.at[2 * chunk + c],
            )
            copy.start()
            outs.append(copy)
    for copy in outs:
        copy.wait()


def local(
    n_lon, n_lat,
    control_fields,
    unexplained_elevation,
    diffusivity,
    depth_levels,
    fold_partner,
    prior_sigmas,
    haline_thermal_ratio,
    expansion_coefficients,
):
    levels, lon_cells, lat_cells = control_fields.shape[1:]
    fields = control_fields.transpose(0, 2, 1, 3)
    partners = jnp.pad(
        fold_partner.reshape(n_lon, lon_cells), ((0, 0), (0, LANES - lon_cells))
    )
    tall = -(-lon_cells // 8) * 8 + 8
    count = lon_cells + 8
    wide = lat_cells + LANES
    f32 = jnp.float32
    vmem = pl.BlockSpec(memory_space=pltpu.VMEM)
    smem = pl.BlockSpec(memory_space=pltpu.SMEM)
    anywhere = pl.BlockSpec(memory_space=pl.ANY)
    halo_shapes = (
        (2, 2, 4, levels, lat_cells),
        (2, 8, lat_cells),
        (2, 8, 4 * LANES),
        (4, 8, 2 * LANES),
        (10, 8, 4 * LANES),
    )
    halos = pl.pallas_call(
        functools.partial(exchange_kernel, n_lon, n_lat),
        name="exchange",
        out_shape=tuple(jax.ShapeDtypeStruct(shape, f32) for shape in halo_shapes),
        in_specs=[anywhere, vmem, vmem],
        out_specs=(anywhere,) * 5,
        scratch_shapes=[
            pltpu.VMEM((2, lon_cells, 8, LANES), f32),
            pltpu.VMEM((8, LANES), f32),
            pltpu.VMEM((2, 8, lat_cells), f32),
            pltpu.VMEM((2, 8, 4 * LANES), f32),
            pltpu.SemaphoreType.DMA((20,)),
            pltpu.SemaphoreType.DMA((20,)),
            pltpu.SemaphoreType.DMA((10,)),
            pltpu.SemaphoreType.DMA((4,)),
        ],
        compiler_params=pltpu.CompilerParams(
            collective_id=0, has_side_effects=True, vmem_limit_bytes=40 * 1024 * 1024
        ),
    )(fields, diffusivity, depth_levels)
    state, height = pl.pallas_call(
        functools.partial(compute_kernel, n_lon, n_lat),
        name="diffuse",
        out_shape=(
            jax.ShapeDtypeStruct(fields.shape, f32),
            jax.ShapeDtypeStruct((lon_cells, lat_cells), f32),
        ),
        in_specs=[anywhere] + [vmem] * 5 + [smem] * 2 + [anywhere] * 5,
        out_specs=(anywhere, vmem),
        scratch_shapes=[
            pltpu.VMEM((count, 8, wide), f32),
            pltpu.VMEM((count, 8, wide), f32),
            pltpu.VMEM((lon_cells, 8, lat_cells), f32),
        ]
        + [pltpu.VMEM((tall, wide), f32)] * 6
        + [pltpu.VMEM((count, 8, wide), f32)] * 2
        + [pltpu.VMEM(shape, f32) for shape in halo_shapes[1:]]
        + [
            pltpu.VMEM((PASSES, 8, LANES), f32),
            pltpu.VMEM((2, LANES + 8, LANES), f32),
            pltpu.SemaphoreType.DMA((10,)),
            pltpu.SemaphoreType.DMA((4,)),
        ],
        compiler_params=pltpu.CompilerParams(vmem_limit_bytes=48 * 1024 * 1024),
    )(
        fields, unexplained_elevation, diffusivity, depth_levels, haline_thermal_ratio,
        partners, prior_sigmas, expansion_coefficients, *halos,
    )
    return state.transpose(0, 2, 1, 3), height


def solution(mesh):
    return jax.shard_map(
        functools.partial(local, mesh.shape["lon"], mesh.shape["lat"]),
        mesh=mesh,
        in_specs=(
            P(None, None, "lon", "lat"),
            P("lon", "lat"),
            P("lon", "lat"),
            P("lon", "lat"),
            P(),
            P(),
            P("lon", "lat"),
            P(),
        ),
        out_specs=(P(None, None, "lon", "lat"), P("lon", "lat")),
        check_vma=False,
    )
```

```python
import functools

import jax
import jax.numpy as jnp
from jax import lax
from jax.experimental import pallas as pl
from jax.experimental.pallas import tpu as pltpu
from jax.sharding import PartitionSpec as P

PASSES = 4
LANES = 128
STRAIGHT_ROWS = (1, 2, 3, 2, 1)
MIRROR_ROWS = (2, 3, 4, 3, 2)
PLACES = (1, 0, 3)
MESH = pl.DeviceIdType.MESH


def unroll_of(trips):
    return max(k for k in range(1, 38) if trips % k == 0)


def exchange_kernel(
    n_lon, n_lat,
    f_ref, k_hbm, d_hbm,
    ew_out, kd_out, p_out, c_out, q_out,
    k_ref, d_ref, edge_buf, tail_buf, kd_buf, p_buf, send_sem, recv_sem, local_sem, load_sem,
):
    lon_cells, lat_cells = k_ref.shape
    b = lax.axis_index("lon")
    a_lat = lax.axis_index("lat")
    has_n = a_lat < n_lat - 1
    has_s = a_lat > 0
    is_top = a_lat == n_lat - 1
    east = lax.rem(b + 1, n_lon)
    west = lax.rem(b + n_lon - 1, n_lon)
    north = lax.rem(a_lat + 1, n_lat)
    south = lax.rem(a_lat + n_lat - 1, n_lat)

    loads = [
        pltpu.make_async_copy(
            f_ref.at[c, :, :, pl.ds(start, LANES)],
            edge_buf.at[side, :, pl.ds(4 * c, 4), :],
            load_sem.at[2 * side + c],
        )
        for side, start in ((0, lat_cells - LANES), (1, 0))
        for c in range(2)
    ]
    bases = [
        pltpu.make_async_copy(k_hbm, k_ref, load_sem.at[4]),
        pltpu.make_async_copy(d_hbm, d_ref, load_sem.at[5]),
    ]
    for copy in bases + loads:
        copy.start()

    straight = [
        (slot, lax.rem(b - (slot - 2) + n_lon, n_lon))
        for slot in (0, 1, 3, 4)
    ]
    mirrored = [
        (5 + slot, lax.rem((slot - 2) - b + 2 * n_lon, n_lon))
        for slot in range(5)
    ]

    barrier = pltpu.get_barrier_semaphore()

    def hail(lon, lat):
        pl.semaphore_signal(
            barrier, inc=1, device_id={"lon": lon, "lat": lat}, device_id_type=MESH
        )

    hail(east, a_lat)
    hail(west, a_lat)

    @pl.when(has_n)
    def _():
        for lon in (west, b, east):
            hail(lon, north)

    @pl.when(has_s)
    def _():
        for lon in (west, b, east):
            hail(lon, south)

    @pl.when(is_top)
    def _():
        for _, target in straight:
            hail(target, a_lat)
        for _, target in mirrored:
            @pl.when(target != b)
            def _():
                hail(target, a_lat)

    expected = 2 + jnp.where(has_n, 3, 0) + jnp.where(has_s, 3, 0) + jnp.where(is_top, 4, 0)
    for _, target in mirrored:
        expected = expected + jnp.where(jnp.logical_and(is_top, target != b), 1, 0)

    def remote(src, dst, index, lon, lat):
        return pltpu.make_async_remote_copy(
            src_ref=src, dst_ref=dst, send_sem=send_sem.at[index], recv_sem=recv_sem.at[index],
            device_id={"lon": lon, "lat": lat}, device_id_type=MESH,
        )

    last = pl.ds(lon_cells - 4, 4)
    first = pl.ds(0, 4)
    far = [
        remote(f_ref.at[:, last], ew_out.at[0], 0, east, a_lat),
        remote(f_ref.at[:, first], ew_out.at[1], 1, west, a_lat),
    ]
    pl.semaphore_wait(barrier, expected)
    for copy in far:
        copy.start()

    for copy in bases:
        copy.wait()
    for source, start in ((k_ref, 0), (d_ref, 4)):
        kd_buf[0, start : start + 4, :] = source[lon_cells - 4 : lon_cells, :].astype(jnp.float32)
        kd_buf[1, start : start + 4, :] = source[0:4, :].astype(jnp.float32)

    lane = lax.broadcasted_iota(jnp.int32, (8, LANES), 1)
    aligned = (lon_cells // 8) * 8
    for side in range(2):
        columns = slice(lat_cells - LANES, lat_cells) if side == 0 else slice(0, LANES)
        offset = 4 if side == 0 else 0
        packed = jnp.zeros((8, LANES), jnp.float32)
        for which, source in enumerate((k_ref, d_ref)):
            tail_buf[...] = jnp.zeros((8, LANES), jnp.float32)
            tail_buf[0 : lon_cells - aligned, :] = source[aligned:lon_cells, columns].astype(jnp.float32)
            for j in range(-(-lon_cells // 8)):
                if 8 * j < aligned:
                    moved = source[8 * j : 8 * j + 8, columns].astype(jnp.float32)
                else:
                    moved = tail_buf[...]
                shift = (8 * j + 4 * which + offset) % LANES
                if shift:
                    moved = pltpu.roll(moved, shift, 1)
                packed = jnp.where(lane // 4 == 2 * j + which, moved, packed)
        p_buf[side, :, 2 * LANES : 3 * LANES] = packed

    for copy in loads:
        copy.wait()
    for side in range(2):
        offset = 4 if side == 0 else 0
        for group in range(3):
            packed = jnp.zeros((8, LANES), jnp.float32)
            for col in range(32 * group, min(32 * group + 32, lon_cells)):
                shift = (4 * (col % 32) + offset) % LANES
                moved = edge_buf[side, col]
                if shift:
                    moved = pltpu.roll(moved, shift, 1)
                packed = jnp.where(lane // 4 == col % 32, moved, packed)
            place = PLACES[group] * LANES
            p_buf[side, :, place : place + LANES] = packed

    along = [
        remote(kd_buf.at[0], kd_out.at[0], 18, east, a_lat),
        remote(kd_buf.at[1], kd_out.at[1], 19, west, a_lat),
    ]
    tail = pl.ds(2 * LANES, 2 * LANES)
    head = pl.ds(LANES, 2 * LANES)
    up = [
        remote(p_buf.at[0], p_out.at[0], 2, b, north),
        remote(p_buf.at[0, :, tail], c_out.at[0], 4, east, north),
        remote(p_buf.at[0, :, head], c_out.at[1], 5, west, north),
    ]
    down = [
        remote(p_buf.at[1], p_out.at[1], 3, b, south),
        remote(p_buf.at[1, :, tail], c_out.at[2], 6, east, south),
        remote(p_buf.at[1, :, head], c_out.at[3], 7, west, south),
    ]

    for copy in along:
        copy.start()

    @pl.when(has_n)
    def _():
        for copy in up:
            copy.start()

    @pl.when(has_s)
    def _():
        for copy in down:
            copy.start()

    strip_straight = [
        remote(p_buf.at[0], q_out.at[slot], 8 + slot, target, a_lat) for slot, target in straight
    ]
    strip_mirrored = [
        (
            target != b,
            remote(p_buf.at[0], q_out.at[slot], 8 + slot, target, a_lat),
            pltpu.make_async_copy(p_buf.at[0], q_out.at[slot], local_sem.at[slot]),
        )
        for slot, target in mirrored
    ]
    own = pltpu.make_async_copy(p_buf.at[0], q_out.at[2], local_sem.at[2])

    @pl.when(is_top)
    def _():
        for copy in strip_straight:
            copy.start()
        for away, copy, stay in strip_mirrored:
            @pl.when(away)
            def _():
                copy.start()

            @pl.when(jnp.logical_not(away))
            def _():
                stay.start()
        own.start()

    for copy in far + along:
        copy.wait_send()
        copy.wait_recv()

    @pl.when(has_n)
    def _():
        for copy in up:
            copy.wait_send()
        for copy in down:
            copy.wait_recv()

    @pl.when(has_s)
    def _():
        for copy in down:
            copy.wait_send()
        for copy in up:
            copy.wait_recv()

    @pl.when(is_top)
    def _():
        for copy in strip_straight:
            copy.wait_send()
            copy.wait_recv()
        for away, copy, stay in strip_mirrored:
            @pl.when(away)
            def _():
                copy.wait_send()
                copy.wait_recv()

            @pl.when(jnp.logical_not(away))
            def _():
                stay.wait()
        own.wait()


def fold_strip(n_lon, lon_cells, b, q_ref, fp_ref, ghost_ref, coast_ref):
    lane = lax.broadcasted_iota(jnp.int32, (8, LANES), 1)
    sublane = lax.broadcasted_iota(jnp.int32, (8, LANES), 0)
    level = (sublane % 4).astype(jnp.float32)

    def spread(row):
        return jnp.broadcast_to(row, (8, LANES))

    def take(values, index):
        return jnp.take_along_axis(values, index, axis=1, mode="promise_in_bounds")

    kinds = {"S": STRAIGHT_ROWS, "M": MIRROR_ROWS}
    field, kappa, depth, index = {}, {}, {}, {}

    def tile(slot, place):
        return q_ref[slot, :, place * LANES : (place + 1) * LANES]

    def column_of(values, start):
        picked = take(values, 8 * (lane // 8) + start)
        return spread(jnp.sum(jnp.where(sublane == lane % 8, picked, 0.0), axis=0, keepdims=True))

    for kind, rows in kinds.items():
        for o in range(-2, 3):
            slot = o + 2 + (0 if kind == "S" else 5)
            block = lax.rem((b if kind == "S" else -b) + o + 2 * n_lon, n_lon)
            opposite = lax.rem(n_lon - block, n_lon)
            index[kind, o] = jnp.maximum(
                spread(fp_ref[pl.ds(block, 1), :]) - opposite * lon_cells, 0
            )
            parts = [tile(slot, place) for place in PLACES]
            meta = tile(slot, 2)
            for r in range(rows[o + 2]):
                kappa[kind, o, r] = column_of(meta, 3 - r)
                depth[kind, o, r] = column_of(meta, 7 - r)
                pieces = [take(part, 4 * (lane % 32) + 3 - r) for part in parts]
                values = jnp.where(
                    lane < 32, pieces[0], jnp.where(lane < 64, pieces[1], pieces[2])
                )
                field[kind, o, r] = jnp.where(depth[kind, o, r] > level, values, 0.0)

    other = {"S": "M", "M": "S"}

    def sides(table, kind, o, r):
        here = table[kind, o, r]
        from_east = table.get((kind, o + 1, r), here)
        from_west = table.get((kind, o - 1, r), here)
        towards = jnp.where(
            lane == lon_cells - 1, pltpu.roll(from_east, lon_cells - 1, 1), pltpu.roll(here, LANES - 1, 1)
        )
        back = jnp.where(
            lane == 0, pltpu.roll(from_west, LANES - lon_cells + 1, 1), pltpu.roll(here, 1, 1)
        )
        return towards, back

    def above(table, kind, o, r):
        if r:
            return table[kind, o, r - 1]
        return take(table[other[kind], -o, 0], index[kind, o])

    faces = {}
    ghosts = []

    def ghost_row(table):
        own = take(table["M", 0, 0], index["S", 0])
        right = take(table["M", -1, 0], index["S", 1])
        left = take(table["M", 1, 0], index["S", -1])
        result = jnp.where(
            lane < 4,
            pltpu.roll(left, (4 - lon_cells) % LANES, 1),
            jnp.where(
                lane < 4 + lon_cells, pltpu.roll(own, 4, 1), pltpu.roll(right, 4 + lon_cells, 1)
            ),
        )
        return jnp.where(lane < 8 + lon_cells, result, 0.0)

    ghost_kappa = ghost_row(kappa)
    ghost_depth = ghost_row(depth)
    ghosts.append(ghost_row(field))
    for step in range(1, PASSES):
        renewed = {}
        for kind, rows in kinds.items():
            for o in range(-2, 3):
                for r in range(rows[o + 2] - step):
                    if (kind, o, r) not in faces:
                        ke, kw = sides(kappa, kind, o, r)
                        de, dw = sides(depth, kind, o, r)
                        kn, dn = above(kappa, kind, o, r), above(depth, kind, o, r)
                        ks, ds = kappa[kind, o, r + 1], depth[kind, o, r + 1]
                        k0, d0 = kappa[kind, o, r], depth[kind, o, r]
                        faces[kind, o, r] = [
                            jnp.where(jnp.minimum(d0, d) > level, k0 * k, 0.0)
                            for k, d in ((ke, de), (kw, dw), (kn, dn), (ks, ds))
                        ]
                    fe, fw, fn, fs = faces[kind, o, r]
                    x = field[kind, o, r]
                    xe, xw = sides(field, kind, o, r)
                    xn = above(field, kind, o, r)
                    xs = field[kind, o, r + 1]
                    renewed[kind, o, r] = (
                        x + fe * (xe - x) + fw * (xw - x) + fn * (xn - x) + fs * (xs - x)
                    )
        field.update(renewed)
        ghosts.append(ghost_row(field))
    for step in range(PASSES):
        ghost_ref[step] = ghosts[step]
    for which, row in ((0, ghost_kappa), (1, ghost_depth)):
        square = jnp.concatenate([row, jnp.zeros((LANES - 8, LANES), jnp.float32)], axis=0).T
        coast_ref[which, 0:4, :] = jnp.zeros((4, LANES), jnp.float32)
        coast_ref[which, 4 : 8 + LANES - 4, :] = square[0:LANES, :]


def compute_kernel(
    n_lon, n_lat,
    f_ref, elev_hbm, k_hbm, d_hbm, ratio_hbm, fp_ref, sigma_hbm, expand_hbm,
    ew_hbm, kd_hbm, p_hbm, c_hbm, q_hbm,
    state_hbm, height_ref,
    elev_ref, k_ref, d_ref, ratio_ref, sigma_ref, expand_ref, xa, xb, ya, kx, dx, lon_k, lon_d, lat_k, lat_d, e_face, n_face,
    kd_ref, p_ref, c_ref, q_ref, ghost_ref, coast_ref, sems, out_sems,
):
    lon_cells, lat_cells = k_ref.shape
    wide = xa.shape[2]
    count = lon_cells + 8
    tall = kx.shape[0]
    b = lax.axis_index("lon")
    a_lat = lax.axis_index("lat")
    is_top = a_lat == n_lat - 1
    is_bottom = a_lat == 0

    small = [
        pltpu.make_async_copy(kd_hbm, kd_ref, sems.at[0]),
        pltpu.make_async_copy(p_hbm, p_ref, sems.at[1]),
        pltpu.make_async_copy(c_hbm, c_ref, sems.at[2]),
        pltpu.make_async_copy(q_hbm, q_ref, sems.at[3]),
    ]
    large = []
    for c in range(2):
        half = pl.ds(4 * c, 4)
        own = pl.ds(0, lat_cells)
        large += [
            pltpu.make_async_copy(ew_hbm.at[0, c], xa.at[pl.ds(0, 4), half, own], sems.at[4 + c]),
            pltpu.make_async_copy(
                ew_hbm.at[1, c], xa.at[pl.ds(lon_cells + 4, 4), half, own], sems.at[6 + c]
            ),
            pltpu.make_async_copy(f_ref.at[c], xa.at[pl.ds(4, lon_cells), half, own], sems.at[8 + c]),
        ]
    base = [
        pltpu.make_async_copy(k_hbm, k_ref, sems.at[10]),
        pltpu.make_async_copy(d_hbm, d_ref, sems.at[11]),
    ]
    late = [
        pltpu.make_async_copy(elev_hbm, elev_ref, sems.at[12]),
        pltpu.make_async_copy(ratio_hbm, ratio_ref, sems.at[13]),
        pltpu.make_async_copy(sigma_hbm, sigma_ref, sems.at[14]),
        pltpu.make_async_copy(expand_hbm, expand_ref, sems.at[15]),
    ]
    for copy in base + small + large + late:
        copy.start()

    sublane = lax.broadcasted_iota(jnp.int32, (8, LANES), 0)
    lane = lax.broadcasted_iota(jnp.int32, (8, LANES), 1)
    for copy in base:
        copy.wait()
    for ref, source in ((kx, k_ref), (dx, d_ref)):
        ref[0:8, :] = jnp.zeros((8, wide), jnp.float32)
        ref[8 : 8 + lon_cells, 0:lat_cells] = source[...].astype(jnp.float32)

    for copy in small:
        copy.wait()

    kx[4:8, 0:lat_cells] = kd_ref[0, 0:4, :]
    dx[4:8, 0:lat_cells] = kd_ref[0, 4:8, :]
    kx[8 + lon_cells : 12 + lon_cells, 0:lat_cells] = kd_ref[1, 0:4, :]
    dx[8 + lon_cells : 12 + lon_cells, 0:lat_cells] = kd_ref[1, 4:8, :]

    def part(ref, place):
        return ref[:, place * LANES : (place + 1) * LANES]

    def clean(present, values):
        return jnp.where(present, values, 0.0)

    no_n, no_s = jnp.logical_not(is_top), jnp.logical_not(is_bottom)
    south = [clean(no_s, part(p_ref.at[0], place)) for place in PLACES]
    north = [clean(no_n, part(p_ref.at[1], place)) for place in PLACES]
    south_west = clean(no_s, part(c_ref.at[0], 1))
    south_east = clean(no_s, part(c_ref.at[1], 0))
    north_west = clean(no_n, part(c_ref.at[2], 1))
    north_east = clean(no_n, part(c_ref.at[3], 0))

    def turned(values, shift):
        shift %= LANES
        return pltpu.roll(values, shift, 1) if shift else values

    def join(up, below, start):
        return jnp.where(
            lane < 4, turned(up, -start),
            jnp.where(lane >= LANES - 4, turned(below, LANES - 4 - start), 0.0),
        )

    for i in range(count):
        if i < 4:
            up, below, at = north_west, south_west, i
        elif i < 4 + lon_cells:
            col = i - 4
            up, below, at = north[col // 32], south[col // 32], col % 32
        else:
            up, below, at = north_east, south_east, i - 4 - lon_cells
        xa[i, :, lat_cells:wide] = join(up, below, 4 * at)

    south_k, north_k = clean(no_s, part(p_ref.at[0], 2)), clean(no_n, part(p_ref.at[1], 2))
    tail_col = (lon_cells // 8) * 8
    corners = (
        (pltpu.roll(clean(no_n, part(c_ref.at[2], 0)), 4, 0), pltpu.roll(clean(no_s, part(c_ref.at[0], 0)), 4, 0)),
        (pltpu.roll(clean(no_n, part(c_ref.at[3], 1)), 4, 0), pltpu.roll(clean(no_s, part(c_ref.at[1], 1)), 4, 0)),
    )
    for which, ref in enumerate((kx, dx)):
        from_west = join(corners[0][0], corners[0][1], tail_col + 4 * which)
        ref[0:8, lat_cells:wide] = jnp.where(sublane >= 4, from_west, 0.0)
        for j in range((tall - 8) // 8):
            piece = join(north_k, south_k, 8 * j + 4 * which)
            if 8 * j == tail_col:
                piece = jnp.where(sublane < 4, piece, join(corners[1][0], corners[1][1], 4 * which))
            ref[8 + 8 * j : 16 + 8 * j, lat_cells:wide] = piece

    @pl.when(is_top)
    def _():
        fold_strip(n_lon, lon_cells, b, q_ref, fp_ref, ghost_ref, coast_ref)
        for which, ref in enumerate((kx, dx)):
            for j in range(tall // 8):
                at = slice(8 * j, 8 * j + 8)
                ref[at, lat_cells:wide] = jnp.where(
                    lane == 0, coast_ref[which, at, :], ref[at, lat_cells:wide]
                )

    for j in range(tall // 8):
        at = slice(8 * j, 8 * j + 8)
        k0, d0 = kx[at, :], dx[at, :]
        lat_k[at, :] = k0 * pltpu.roll(k0, wide - 1, 1)
        lat_d[at, :] = jnp.minimum(d0, pltpu.roll(d0, wide - 1, 1))
        if j < tall // 8 - 1:
            after = slice(8 * j + 1, 8 * j + 9)
            lon_k[at, :] = k0 * kx[after, :]
            lon_d[at, :] = jnp.minimum(d0, dx[after, :])
        else:
            after = slice(8 * j + 1, 8 * j + 8)
            at = slice(8 * j, 8 * j + 7)
            lon_k[at, :] = kx[at, :] * kx[after, :]
            lon_d[at, :] = jnp.minimum(dx[at, :], dx[after, :])
            lon_k[tall - 1 : tall, :] = jnp.zeros((1, wide), jnp.float32)
            lon_d[tall - 1 : tall, :] = jnp.zeros((1, wide), jnp.float32)

    level = (lax.broadcasted_iota(jnp.int32, (8, wide), 0) % 4).astype(jnp.float32)

    def row(ref, i):
        return jnp.broadcast_to(ref[pl.ds(i + 4, 1), :], (8, ref.shape[1]))

    def make_faces(i, carry):
        e_face[i] = jnp.where(row(lon_d, i) > level, row(lon_k, i), 0.0)
        n_face[i] = jnp.where(row(lat_d, i) > level, row(lat_k, i), 0.0)
        return carry

    lax.fori_loop(0, count, make_faces, 0, unroll=unroll_of(count))

    for copy in large:
        copy.wait()

    def mask(i, carry):
        xa[i] = jnp.where(row(dx, i) > level, xa[i], 0.0)
        return carry

    lax.fori_loop(0, count, mask, 0, unroll=unroll_of(count))

    def advance(source, i, state):
        x, flux_west = state
        x_east = source[i + 1]
        flux_east = e_face[i] * (x_east - x)
        flux_north = n_face[i] * (pltpu.roll(x, wide - 1, 1) - x)
        fresh = ((x + flux_east) - flux_west) + (flux_north - pltpu.roll(flux_north, 1, 1))
        return fresh, (x_east, flux_east)

    def refresh(ref, step):
        @pl.when(is_top)
        def _():
            ghosts = ghost_ref[step]
            for i in range(step + 1, count - step - 1):
                ref[i, :, lat_cells:wide] = jnp.where(
                    lane == 0, turned(ghosts, -i), ref[i, :, lat_cells:wide]
                )

    def start_of(source, first):
        x = source[first]
        return x, e_face[first - 1] * (x - source[first - 1])

    source, target = xa, xb
    for step in range(PASSES - 1):
        refresh(source, step)
        first, stop = step + 1, count - step - 1

        def one(i, state, source=source, target=target):
            fresh, state = advance(source, i, state)
            target[i] = fresh
            return state

        lax.fori_loop(first, stop, one, start_of(source, first), unroll=unroll_of(stop - first))
        source, target = target, source
    refresh(source, PASSES - 1)

    for copy in late:
        copy.wait()
    short = lax.broadcasted_iota(jnp.int32, (8, lat_cells), 0)
    sigma = jnp.zeros((8, lat_cells), jnp.float32)
    expand = jnp.zeros((8, lat_cells), jnp.float32)
    for c in range(2):
        for k in range(4):
            sigma = jnp.where(short == 4 * c + k, sigma_ref[c, k], sigma)
            expand = jnp.where(short == 4 * c + k, expand_ref[c, k], expand)

    def balance(i, state):
        fresh, state = advance(source, i, state)
        scaled = sigma * fresh[:, 0:lat_cells]
        col = i - 4
        ratio = jnp.broadcast_to(ratio_ref[pl.ds(col, 1), :], (8, lat_cells))
        result = scaled + jnp.where(short >= 4, ratio * pltpu.roll(scaled, 4, 0), 0.0)
        ya[col] = result
        height_ref[pl.ds(col, 1), :] = elev_ref[pl.ds(col, 1), :] + jnp.sum(
            expand * result, axis=0, keepdims=True
        )
        return state

    state = start_of(source, 4)
    middle = (lon_cells // 4) * 2
    bounds = (0, middle, lon_cells)
    outs = []
    for chunk in range(2):
        lo, hi = bounds[chunk], bounds[chunk + 1]
        state = lax.fori_loop(lo + 4, hi + 4, balance, state, unroll=unroll_of((hi - lo) // 2))
        for c in range(2):
            copy = pltpu.make_async_copy(
                ya.at[pl.ds(lo, hi - lo), pl.ds(4 * c, 4), :],
                state_hbm.at[c, pl.ds(lo, hi - lo)],
                out_sems.at[2 * chunk + c],
            )
            copy.start()
            outs.append(copy)
    for copy in outs:
        copy.wait()


def local(
    n_lon, n_lat,
    control_fields,
    unexplained_elevation,
    diffusivity,
    depth_levels,
    fold_partner,
    prior_sigmas,
    haline_thermal_ratio,
    expansion_coefficients,
):
    levels, lon_cells, lat_cells = control_fields.shape[1:]
    fields = control_fields.transpose(0, 2, 1, 3)
    partners = jnp.pad(
        fold_partner.reshape(n_lon, lon_cells), ((0, 0), (0, LANES - lon_cells))
    )
    tall = -(-lon_cells // 8) * 8 + 8
    count = lon_cells + 8
    wide = lat_cells + LANES
    f32 = jnp.float32
    vmem = pl.BlockSpec(memory_space=pltpu.VMEM)
    hbm = pl.BlockSpec(memory_space=pltpu.HBM)
    anywhere = pl.BlockSpec(memory_space=pl.ANY)
    halo_shapes = (
        (2, 2, 4, levels, lat_cells),
        (2, 8, lat_cells),
        (2, 8, 4 * LANES),
        (4, 8, 2 * LANES),
        (10, 8, 4 * LANES),
    )
    halos = pl.pallas_call(
        functools.partial(exchange_kernel, n_lon, n_lat),
        name="exchange",
        out_shape=tuple(jax.ShapeDtypeStruct(shape, f32) for shape in halo_shapes),
        in_specs=[hbm] * 3,
        out_specs=(anywhere,) * 5,
        scratch_shapes=[
            pltpu.VMEM((lon_cells, lat_cells), f32),
            pltpu.VMEM((lon_cells, lat_cells), jnp.int32),
            pltpu.VMEM((2, lon_cells, 8, LANES), f32),
            pltpu.VMEM((8, LANES), f32),
            pltpu.VMEM((2, 8, lat_cells), f32),
            pltpu.VMEM((2, 8, 4 * LANES), f32),
            pltpu.SemaphoreType.DMA((20,)),
            pltpu.SemaphoreType.DMA((20,)),
            pltpu.SemaphoreType.DMA((10,)),
            pltpu.SemaphoreType.DMA((6,)),
        ],
        compiler_params=pltpu.CompilerParams(
            collective_id=0, has_side_effects=True, vmem_limit_bytes=63 * 1024 * 1024
        ),
    )(fields, diffusivity, depth_levels)
    state, height = pl.pallas_call(
        functools.partial(compute_kernel, n_lon, n_lat),
        name="diffuse",
        out_shape=(
            jax.ShapeDtypeStruct(fields.shape, f32),
            jax.ShapeDtypeStruct((lon_cells, lat_cells), f32),
        ),
        in_specs=[hbm] * 5 + [vmem] + [hbm] * 2 + [anywhere] * 5,
        out_specs=(anywhere, vmem),
        scratch_shapes=[
            pltpu.VMEM((lon_cells, lat_cells), f32),
            pltpu.VMEM((lon_cells, lat_cells), f32),
            pltpu.VMEM((lon_cells, lat_cells), jnp.int32),
            pltpu.VMEM((lon_cells, lat_cells), f32),
            pltpu.SMEM((2, levels), f32),
            pltpu.SMEM((2, levels), f32),
            pltpu.VMEM((count, 8, wide), f32),
            pltpu.VMEM((count, 8, wide), f32),
            pltpu.VMEM((lon_cells, 8, lat_cells), f32),
        ]
        + [pltpu.VMEM((tall, wide), f32)] * 6
        + [pltpu.VMEM((count, 8, wide), f32)] * 2
        + [pltpu.VMEM(shape, f32) for shape in halo_shapes[1:]]
        + [
            pltpu.VMEM((PASSES, 8, LANES), f32),
            pltpu.VMEM((2, LANES + 8, LANES), f32),
            pltpu.SemaphoreType.DMA((16,)),
            pltpu.SemaphoreType.DMA((4,)),
        ],
        compiler_params=pltpu.CompilerParams(vmem_limit_bytes=63 * 1024 * 1024),
    )(
        fields, unexplained_elevation, diffusivity, depth_levels, haline_thermal_ratio,
        partners, prior_sigmas, expansion_coefficients, *halos,
    )
    return state.transpose(0, 2, 1, 3), height


def solution(mesh):
    return jax.shard_map(
        functools.partial(local, mesh.shape["lon"], mesh.shape["lat"]),
        mesh=mesh,
        in_specs=(
            P(None, None, "lon", "lat"),
            P("lon", "lat"),
            P("lon", "lat"),
            P("lon", "lat"),
            P(),
            P(),
            P("lon", "lat"),
            P(),
        ),
        out_specs=(P(None, None, "lon", "lat"), P("lon", "lat")),
        check_vma=False,
    )
```

```python
import functools

import jax
import jax.numpy as jnp
from jax import lax
from jax.experimental import pallas as pl
from jax.experimental.pallas import tpu as pltpu
from jax.sharding import PartitionSpec as P

PASSES = 4
LANES = 128
STRAIGHT_ROWS = (1, 2, 3, 2, 1)
MIRROR_ROWS = (2, 3, 4, 3, 2)
PLACES = (1, 0, 3)
MESH = pl.DeviceIdType.MESH


def unrolled(first, stop, body, state):
    for i in range(first, stop):
        state = body(i, state)
    return state


def exchange_kernel(
    n_lon, n_lat,
    f_ref, k_hbm, d_hbm,
    ew_out, kd_out, p_out, c_out, q_out,
    k_ref, d_ref, edge_buf, tail_buf, kd_buf, p_buf, send_sem, recv_sem, local_sem, load_sem,
):
    lon_cells, lat_cells = k_ref.shape
    b = lax.axis_index("lon")
    a_lat = lax.axis_index("lat")
    has_n = a_lat < n_lat - 1
    has_s = a_lat > 0
    is_top = a_lat == n_lat - 1
    east = lax.rem(b + 1, n_lon)
    west = lax.rem(b + n_lon - 1, n_lon)
    north = lax.rem(a_lat + 1, n_lat)
    south = lax.rem(a_lat + n_lat - 1, n_lat)

    loads = [
        pltpu.make_async_copy(
            f_ref.at[c, :, :, pl.ds(start, LANES)],
            edge_buf.at[side, :, pl.ds(4 * c, 4), :],
            load_sem.at[2 * side + c],
        )
        for side, start in ((0, lat_cells - LANES), (1, 0))
        for c in range(2)
    ]
    bases = [
        pltpu.make_async_copy(k_hbm, k_ref, load_sem.at[4]),
        pltpu.make_async_copy(d_hbm, d_ref, load_sem.at[5]),
    ]
    for copy in bases + loads:
        copy.start()

    straight = [
        (slot, lax.rem(b - (slot - 2) + n_lon, n_lon))
        for slot in (0, 1, 3, 4)
    ]
    mirrored = [
        (5 + slot, lax.rem((slot - 2) - b + 2 * n_lon, n_lon))
        for slot in range(5)
    ]

    barrier = pltpu.get_barrier_semaphore()

    def hail(lon, lat):
        pl.semaphore_signal(
            barrier, inc=1, device_id={"lon": lon, "lat": lat}, device_id_type=MESH
        )

    hail(east, a_lat)
    hail(west, a_lat)

    @pl.when(has_n)
    def _():
        for lon in (west, b, east):
            hail(lon, north)

    @pl.when(has_s)
    def _():
        for lon in (west, b, east):
            hail(lon, south)

    @pl.when(is_top)
    def _():
        for _, target in straight:
            hail(target, a_lat)
        for _, target in mirrored:
            @pl.when(target != b)
            def _():
                hail(target, a_lat)

    expected = 2 + jnp.where(has_n, 3, 0) + jnp.where(has_s, 3, 0) + jnp.where(is_top, 4, 0)
    for _, target in mirrored:
        expected = expected + jnp.where(jnp.logical_and(is_top, target != b), 1, 0)

    def remote(src, dst, index, lon, lat):
        return pltpu.make_async_remote_copy(
            src_ref=src, dst_ref=dst, send_sem=send_sem.at[index], recv_sem=recv_sem.at[index],
            device_id={"lon": lon, "lat": lat}, device_id_type=MESH,
        )

    last = pl.ds(lon_cells - 4, 4)
    first = pl.ds(0, 4)
    far = [
        remote(f_ref.at[:, last], ew_out.at[0], 0, east, a_lat),
        remote(f_ref.at[:, first], ew_out.at[1], 1, west, a_lat),
    ]
    pl.semaphore_wait(barrier, expected)
    for copy in far:
        copy.start()

    for copy in bases:
        copy.wait()
    for source, start in ((k_ref, 0), (d_ref, 4)):
        kd_buf[0, start : start + 4, :] = source[lon_cells - 4 : lon_cells, :].astype(jnp.float32)
        kd_buf[1, start : start + 4, :] = source[0:4, :].astype(jnp.float32)

    lane = lax.broadcasted_iota(jnp.int32, (8, LANES), 1)
    aligned = (lon_cells // 8) * 8
    for side in range(2):
        columns = slice(lat_cells - LANES, lat_cells) if side == 0 else slice(0, LANES)
        offset = 4 if side == 0 else 0
        packed = jnp.zeros((8, LANES), jnp.float32)
        for which, source in enumerate((k_ref, d_ref)):
            tail_buf[...] = jnp.zeros((8, LANES), jnp.float32)
            tail_buf[0 : lon_cells - aligned, :] = source[aligned:lon_cells, columns].astype(jnp.float32)
            for j in range(-(-lon_cells // 8)):
                if 8 * j < aligned:
                    moved = source[8 * j : 8 * j + 8, columns].astype(jnp.float32)
                else:
                    moved = tail_buf[...]
                shift = (8 * j + 4 * which + offset) % LANES
                if shift:
                    moved = pltpu.roll(moved, shift, 1)
                packed = jnp.where(lane // 4 == 2 * j + which, moved, packed)
        p_buf[side, :, 2 * LANES : 3 * LANES] = packed

    for copy in loads:
        copy.wait()
    for side in range(2):
        offset = 4 if side == 0 else 0
        for group in range(3):
            packed = jnp.zeros((8, LANES), jnp.float32)
            for col in range(32 * group, min(32 * group + 32, lon_cells)):
                shift = (4 * (col % 32) + offset) % LANES
                moved = edge_buf[side, col]
                if shift:
                    moved = pltpu.roll(moved, shift, 1)
                packed = jnp.where(lane // 4 == col % 32, moved, packed)
            place = PLACES[group] * LANES
            p_buf[side, :, place : place + LANES] = packed

    along = [
        remote(kd_buf.at[0], kd_out.at[0], 18, east, a_lat),
        remote(kd_buf.at[1], kd_out.at[1], 19, west, a_lat),
    ]
    tail = pl.ds(2 * LANES, 2 * LANES)
    head = pl.ds(LANES, 2 * LANES)
    up = [
        remote(p_buf.at[0], p_out.at[0], 2, b, north),
        remote(p_buf.at[0, :, tail], c_out.at[0], 4, east, north),
        remote(p_buf.at[0, :, head], c_out.at[1], 5, west, north),
    ]
    down = [
        remote(p_buf.at[1], p_out.at[1], 3, b, south),
        remote(p_buf.at[1, :, tail], c_out.at[2], 6, east, south),
        remote(p_buf.at[1, :, head], c_out.at[3], 7, west, south),
    ]

    for copy in along:
        copy.start()

    @pl.when(has_n)
    def _():
        for copy in up:
            copy.start()

    @pl.when(has_s)
    def _():
        for copy in down:
            copy.start()

    strip_straight = [
        remote(p_buf.at[0], q_out.at[slot], 8 + slot, target, a_lat) for slot, target in straight
    ]
    strip_mirrored = [
        (
            target != b,
            remote(p_buf.at[0], q_out.at[slot], 8 + slot, target, a_lat),
            pltpu.make_async_copy(p_buf.at[0], q_out.at[slot], local_sem.at[slot]),
        )
        for slot, target in mirrored
    ]
    own = pltpu.make_async_copy(p_buf.at[0], q_out.at[2], local_sem.at[2])

    @pl.when(is_top)
    def _():
        for copy in strip_straight:
            copy.start()
        for away, copy, stay in strip_mirrored:
            @pl.when(away)
            def _():
                copy.start()

            @pl.when(jnp.logical_not(away))
            def _():
                stay.start()
        own.start()

    for copy in far + along:
        copy.wait_send()
        copy.wait_recv()

    @pl.when(has_n)
    def _():
        for copy in up:
            copy.wait_send()
        for copy in down:
            copy.wait_recv()

    @pl.when(has_s)
    def _():
        for copy in down:
            copy.wait_send()
        for copy in up:
            copy.wait_recv()

    @pl.when(is_top)
    def _():
        for copy in strip_straight:
            copy.wait_send()
            copy.wait_recv()
        for away, copy, stay in strip_mirrored:
            @pl.when(away)
            def _():
                copy.wait_send()
                copy.wait_recv()

            @pl.when(jnp.logical_not(away))
            def _():
                stay.wait()
        own.wait()


def fold_strip(n_lon, lon_cells, b, q_ref, fp_ref, ghost_ref, coast_ref):
    lane = lax.broadcasted_iota(jnp.int32, (8, LANES), 1)
    sublane = lax.broadcasted_iota(jnp.int32, (8, LANES), 0)
    level = (sublane % 4).astype(jnp.float32)

    def spread(row):
        return jnp.broadcast_to(row, (8, LANES))

    def take(values, index):
        return jnp.take_along_axis(values, index, axis=1, mode="promise_in_bounds")

    kinds = {"S": STRAIGHT_ROWS, "M": MIRROR_ROWS}
    field, kappa, depth, index = {}, {}, {}, {}

    def tile(slot, place):
        return q_ref[slot, :, place * LANES : (place + 1) * LANES]

    def column_of(values, start):
        picked = take(values, 8 * (lane // 8) + start)
        return spread(jnp.sum(jnp.where(sublane == lane % 8, picked, 0.0), axis=0, keepdims=True))

    for kind, rows in kinds.items():
        for o in range(-2, 3):
            slot = o + 2 + (0 if kind == "S" else 5)
            block = lax.rem((b if kind == "S" else -b) + o + 2 * n_lon, n_lon)
            opposite = lax.rem(n_lon - block, n_lon)
            index[kind, o] = jnp.maximum(
                spread(fp_ref[pl.ds(block, 1), :]) - opposite * lon_cells, 0
            )
            parts = [tile(slot, place) for place in PLACES]
            meta = tile(slot, 2)
            for r in range(rows[o + 2]):
                kappa[kind, o, r] = column_of(meta, 3 - r)
                depth[kind, o, r] = column_of(meta, 7 - r)
                pieces = [take(part, 4 * (lane % 32) + 3 - r) for part in parts]
                values = jnp.where(
                    lane < 32, pieces[0], jnp.where(lane < 64, pieces[1], pieces[2])
                )
                field[kind, o, r] = jnp.where(depth[kind, o, r] > level, values, 0.0)

    other = {"S": "M", "M": "S"}

    def sides(table, kind, o, r):
        here = table[kind, o, r]
        from_east = table.get((kind, o + 1, r), here)
        from_west = table.get((kind, o - 1, r), here)
        towards = jnp.where(
            lane == lon_cells - 1, pltpu.roll(from_east, lon_cells - 1, 1), pltpu.roll(here, LANES - 1, 1)
        )
        back = jnp.where(
            lane == 0, pltpu.roll(from_west, LANES - lon_cells + 1, 1), pltpu.roll(here, 1, 1)
        )
        return towards, back

    def above(table, kind, o, r):
        if r:
            return table[kind, o, r - 1]
        return take(table[other[kind], -o, 0], index[kind, o])

    faces = {}
    ghosts = []

    def ghost_row(table):
        own = take(table["M", 0, 0], index["S", 0])
        right = take(table["M", -1, 0], index["S", 1])
        left = take(table["M", 1, 0], index["S", -1])
        result = jnp.where(
            lane < 4,
            pltpu.roll(left, (4 - lon_cells) % LANES, 1),
            jnp.where(
                lane < 4 + lon_cells, pltpu.roll(own, 4, 1), pltpu.roll(right, 4 + lon_cells, 1)
            ),
        )
        return jnp.where(lane < 8 + lon_cells, result, 0.0)

    ghost_kappa = ghost_row(kappa)
    ghost_depth = ghost_row(depth)
    ghosts.append(ghost_row(field))
    for step in range(1, PASSES):
        renewed = {}
        for kind, rows in kinds.items():
            for o in range(-2, 3):
                for r in range(rows[o + 2] - step):
                    if (kind, o, r) not in faces:
                        ke, kw = sides(kappa, kind, o, r)
                        de, dw = sides(depth, kind, o, r)
                        kn, dn = above(kappa, kind, o, r), above(depth, kind, o, r)
                        ks, ds = kappa[kind, o, r + 1], depth[kind, o, r + 1]
                        k0, d0 = kappa[kind, o, r], depth[kind, o, r]
                        faces[kind, o, r] = [
                            jnp.where(jnp.minimum(d0, d) > level, k0 * k, 0.0)
                            for k, d in ((ke, de), (kw, dw), (kn, dn), (ks, ds))
                        ]
                    fe, fw, fn, fs = faces[kind, o, r]
                    x = field[kind, o, r]
                    xe, xw = sides(field, kind, o, r)
                    xn = above(field, kind, o, r)
                    xs = field[kind, o, r + 1]
                    renewed[kind, o, r] = (
                        x + fe * (xe - x) + fw * (xw - x) + fn * (xn - x) + fs * (xs - x)
                    )
        field.update(renewed)
        ghosts.append(ghost_row(field))
    for step in range(PASSES):
        ghost_ref[step] = ghosts[step]
    for which, row in ((0, ghost_kappa), (1, ghost_depth)):
        square = jnp.concatenate([row, jnp.zeros((LANES - 8, LANES), jnp.float32)], axis=0).T
        coast_ref[which, 0:4, :] = jnp.zeros((4, LANES), jnp.float32)
        coast_ref[which, 4 : 8 + LANES - 4, :] = square[0:LANES, :]


def compute_kernel(
    n_lon, n_lat,
    f_ref, elev_hbm, k_hbm, d_hbm, ratio_hbm, fp_ref, sigma_hbm, expand_hbm,
    ew_hbm, kd_hbm, p_hbm, c_hbm, q_hbm,
    state_hbm, height_ref,
    elev_ref, k_ref, d_ref, ratio_ref, sigma_ref, expand_ref, xa, xb, raw, ew_ref, kx, dx, lon_k, lon_d, lat_k, lat_d, e_face, n_face,
    kd_ref, p_ref, c_ref, q_ref, ghost_ref, coast_ref, sems, out_sems,
):
    lon_cells, lat_cells = k_ref.shape
    wide = xa.shape[2]
    count = lon_cells + 8
    tall = kx.shape[0]
    b = lax.axis_index("lon")
    a_lat = lax.axis_index("lat")
    is_top = a_lat == n_lat - 1
    is_bottom = a_lat == 0

    small = [
        pltpu.make_async_copy(kd_hbm, kd_ref, sems.at[0]),
        pltpu.make_async_copy(p_hbm, p_ref, sems.at[1]),
        pltpu.make_async_copy(c_hbm, c_ref, sems.at[2]),
        pltpu.make_async_copy(q_hbm, q_ref, sems.at[3]),
    ]
    large = [
        pltpu.make_async_copy(ew_hbm, ew_ref, sems.at[4]),
        pltpu.make_async_copy(f_ref, raw, sems.at[5]),
    ]
    base = [
        pltpu.make_async_copy(k_hbm, k_ref, sems.at[10]),
        pltpu.make_async_copy(d_hbm, d_ref, sems.at[11]),
    ]
    late = [
        pltpu.make_async_copy(elev_hbm, elev_ref, sems.at[12]),
        pltpu.make_async_copy(ratio_hbm, ratio_ref, sems.at[13]),
        pltpu.make_async_copy(sigma_hbm, sigma_ref, sems.at[14]),
        pltpu.make_async_copy(expand_hbm, expand_ref, sems.at[15]),
    ]
    for copy in base + small + large + late:
        copy.start()

    sublane = lax.broadcasted_iota(jnp.int32, (8, LANES), 0)
    lane = lax.broadcasted_iota(jnp.int32, (8, LANES), 1)
    for copy in base:
        copy.wait()
    for ref, source in ((kx, k_ref), (dx, d_ref)):
        ref[0:8, :] = jnp.zeros((8, wide), jnp.float32)
        ref[8 : 8 + lon_cells, 0:lat_cells] = source[...].astype(jnp.float32)

    for copy in small:
        copy.wait()

    kx[4:8, 0:lat_cells] = kd_ref[0, 0:4, :]
    dx[4:8, 0:lat_cells] = kd_ref[0, 4:8, :]
    kx[8 + lon_cells : 12 + lon_cells, 0:lat_cells] = kd_ref[1, 0:4, :]
    dx[8 + lon_cells : 12 + lon_cells, 0:lat_cells] = kd_ref[1, 4:8, :]

    def part(ref, place):
        return ref[:, place * LANES : (place + 1) * LANES]

    def clean(present, values):
        return jnp.where(present, values, 0.0)

    no_n, no_s = jnp.logical_not(is_top), jnp.logical_not(is_bottom)
    south = [clean(no_s, part(p_ref.at[0], place)) for place in PLACES]
    north = [clean(no_n, part(p_ref.at[1], place)) for place in PLACES]
    south_west = clean(no_s, part(c_ref.at[0], 1))
    south_east = clean(no_s, part(c_ref.at[1], 0))
    north_west = clean(no_n, part(c_ref.at[2], 1))
    north_east = clean(no_n, part(c_ref.at[3], 0))

    def turned(values, shift):
        shift %= LANES
        return pltpu.roll(values, shift, 1) if shift else values

    def join(up, below, start):
        return jnp.where(
            lane < 4, turned(up, -start),
            jnp.where(lane >= LANES - 4, turned(below, LANES - 4 - start), 0.0),
        )

    for i in range(count):
        if i < 4:
            up, below, at = north_west, south_west, i
        elif i < 4 + lon_cells:
            col = i - 4
            up, below, at = north[col // 32], south[col // 32], col % 32
        else:
            up, below, at = north_east, south_east, i - 4 - lon_cells
        xa[i, :, lat_cells:wide] = join(up, below, 4 * at)

    south_k, north_k = clean(no_s, part(p_ref.at[0], 2)), clean(no_n, part(p_ref.at[1], 2))
    tail_col = (lon_cells // 8) * 8
    corners = (
        (pltpu.roll(clean(no_n, part(c_ref.at[2], 0)), 4, 0), pltpu.roll(clean(no_s, part(c_ref.at[0], 0)), 4, 0)),
        (pltpu.roll(clean(no_n, part(c_ref.at[3], 1)), 4, 0), pltpu.roll(clean(no_s, part(c_ref.at[1], 1)), 4, 0)),
    )
    for which, ref in enumerate((kx, dx)):
        from_west = join(corners[0][0], corners[0][1], tail_col + 4 * which)
        ref[0:8, lat_cells:wide] = jnp.where(sublane >= 4, from_west, 0.0)
        for j in range((tall - 8) // 8):
            piece = join(north_k, south_k, 8 * j + 4 * which)
            if 8 * j == tail_col:
                piece = jnp.where(sublane < 4, piece, join(corners[1][0], corners[1][1], 4 * which))
            ref[8 + 8 * j : 16 + 8 * j, lat_cells:wide] = piece

    @pl.when(is_top)
    def _():
        fold_strip(n_lon, lon_cells, b, q_ref, fp_ref, ghost_ref, coast_ref)
        for which, ref in enumerate((kx, dx)):
            for j in range(tall // 8):
                at = slice(8 * j, 8 * j + 8)
                ref[at, lat_cells:wide] = jnp.where(
                    lane == 0, coast_ref[which, at, :], ref[at, lat_cells:wide]
                )

    for j in range(tall // 8):
        at = slice(8 * j, 8 * j + 8)
        k0, d0 = kx[at, :], dx[at, :]
        lat_k[at, :] = k0 * pltpu.roll(k0, wide - 1, 1)
        lat_d[at, :] = jnp.minimum(d0, pltpu.roll(d0, wide - 1, 1))
        if j < tall // 8 - 1:
            after = slice(8 * j + 1, 8 * j + 9)
            lon_k[at, :] = k0 * kx[after, :]
            lon_d[at, :] = jnp.minimum(d0, dx[after, :])
        else:
            after = slice(8 * j + 1, 8 * j + 8)
            at = slice(8 * j, 8 * j + 7)
            lon_k[at, :] = kx[at, :] * kx[after, :]
            lon_d[at, :] = jnp.minimum(dx[at, :], dx[after, :])
            lon_k[tall - 1 : tall, :] = jnp.zeros((1, wide), jnp.float32)
            lon_d[tall - 1 : tall, :] = jnp.zeros((1, wide), jnp.float32)

    level = (lax.broadcasted_iota(jnp.int32, (8, wide), 0) % 4).astype(jnp.float32)

    def row(ref, i):
        return jnp.broadcast_to(ref[pl.ds(i + 4, 1), :], (8, ref.shape[1]))

    def make_faces(i, carry):
        e_face[i] = jnp.where(row(lon_d, i) > level, row(lon_k, i), 0.0)
        n_face[i] = jnp.where(row(lat_d, i) > level, row(lat_k, i), 0.0)
        return carry

    unrolled(0, count, make_faces, 0)

    for copy in large:
        copy.wait()

    def mask(i, where_from):
        wet = row(dx, i) > level
        pair = jnp.concatenate([where_from[0], where_from[1]], axis=0)
        xa[i, :, 0:lat_cells] = jnp.where(wet[:, 0:lat_cells], pair, 0.0)
        xa[i, :, lat_cells:wide] = jnp.where(wet[:, lat_cells:wide], xa[i, :, lat_cells:wide], 0.0)

    for i in range(4):
        mask(i, (ew_ref[0, 0, i], ew_ref[0, 1, i]))
        mask(lon_cells + 4 + i, (ew_ref[1, 0, i], ew_ref[1, 1, i]))

    def mask_own(col, carry):
        mask(col + 4, (raw[0, col], raw[1, col]))
        return carry

    unrolled(0, lon_cells, mask_own, 0)

    def advance(source, i, state):
        x, flux_west = state
        x_east = source[i + 1]
        flux_east = e_face[i] * (x_east - x)
        flux_north = n_face[i] * (pltpu.roll(x, wide - 1, 1) - x)
        fresh = ((x + flux_east) - flux_west) + (flux_north - pltpu.roll(flux_north, 1, 1))
        return fresh, (x_east, flux_east)

    def refresh(ref, step):
        @pl.when(is_top)
        def _():
            ghosts = ghost_ref[step]
            for i in range(step + 1, count - step - 1):
                ref[i, :, lat_cells:wide] = jnp.where(
                    lane == 0, turned(ghosts, -i), ref[i, :, lat_cells:wide]
                )

    def start_of(source, first):
        x = source[first]
        return x, e_face[first - 1] * (x - source[first - 1])

    source, target = xa, xb
    for step in range(PASSES - 1):
        refresh(source, step)
        first, stop = step + 1, count - step - 1

        def one(i, state, source=source, target=target):
            fresh, state = advance(source, i, state)
            target[i] = fresh
            return state

        unrolled(first, stop, one, start_of(source, first))
        source, target = target, source
    refresh(source, PASSES - 1)

    for copy in late:
        copy.wait()
    short = lax.broadcasted_iota(jnp.int32, (8, lat_cells), 0)
    sigma = jnp.zeros((8, lat_cells), jnp.float32)
    expand = jnp.zeros((8, lat_cells), jnp.float32)
    for c in range(2):
        for k in range(4):
            sigma = jnp.where(short == 4 * c + k, sigma_ref[c, k], sigma)
            expand = jnp.where(short == 4 * c + k, expand_ref[c, k], expand)

    def balance(i, state):
        fresh, state = advance(source, i, state)
        scaled = sigma * fresh[:, 0:lat_cells]
        col = i - 4
        ratio = jnp.broadcast_to(ratio_ref[pl.ds(col, 1), :], (8, lat_cells))
        result = scaled + jnp.where(short >= 4, ratio * pltpu.roll(scaled, 4, 0), 0.0)
        raw[0, col] = result[0:4]
        raw[1, col] = result[4:8]
        height_ref[pl.ds(col, 1), :] = elev_ref[pl.ds(col, 1), :] + jnp.sum(
            expand * result, axis=0, keepdims=True
        )
        return state

    state = start_of(source, 4)
    middle = (lon_cells // 4) * 2
    bounds = (0, middle, lon_cells)
    outs = []
    for chunk in range(2):
        lo, hi = bounds[chunk], bounds[chunk + 1]
        state = unrolled(lo + 4, hi + 4, balance, state)
        part_of = pl.ds(lo, hi - lo)
        copy = pltpu.make_async_copy(
            raw.at[:, part_of], state_hbm.at[:, part_of], out_sems.at[chunk]
        )
        copy.start()
        outs.append(copy)
    for copy in outs:
        copy.wait()


def local(
    n_lon, n_lat,
    control_fields,
    unexplained_elevation,
    diffusivity,
    depth_levels,
    fold_partner,
    prior_sigmas,
    haline_thermal_ratio,
    expansion_coefficients,
):
    levels, lon_cells, lat_cells = control_fields.shape[1:]
    fields = control_fields.transpose(0, 2, 1, 3)
    partners = jnp.pad(
        fold_partner.reshape(n_lon, lon_cells), ((0, 0), (0, LANES - lon_cells))
    )
    tall = -(-lon_cells // 8) * 8 + 8
    count = lon_cells + 8
    wide = lat_cells + LANES
    f32 = jnp.float32
    vmem = pl.BlockSpec(memory_space=pltpu.VMEM)
    hbm = pl.BlockSpec(memory_space=pltpu.HBM)
    anywhere = pl.BlockSpec(memory_space=pl.ANY)
    halo_shapes = (
        (2, 2, 4, levels, lat_cells),
        (2, 8, lat_cells),
        (2, 8, 4 * LANES),
        (4, 8, 2 * LANES),
        (10, 8, 4 * LANES),
    )
    halos = pl.pallas_call(
        functools.partial(exchange_kernel, n_lon, n_lat),
        name="exchange",
        out_shape=tuple(jax.ShapeDtypeStruct(shape, f32) for shape in halo_shapes),
        in_specs=[hbm] * 3,
        out_specs=(anywhere,) * 5,
        scratch_shapes=[
            pltpu.VMEM((lon_cells, lat_cells), f32),
            pltpu.VMEM((lon_cells, lat_cells), jnp.int32),
            pltpu.VMEM((2, lon_cells, 8, LANES), f32),
            pltpu.VMEM((8, LANES), f32),
            pltpu.VMEM((2, 8, lat_cells), f32),
            pltpu.VMEM((2, 8, 4 * LANES), f32),
            pltpu.SemaphoreType.DMA((20,)),
            pltpu.SemaphoreType.DMA((20,)),
            pltpu.SemaphoreType.DMA((10,)),
            pltpu.SemaphoreType.DMA((6,)),
        ],
        compiler_params=pltpu.CompilerParams(
            collective_id=0, has_side_effects=True, vmem_limit_bytes=63 * 1024 * 1024
        ),
    )(fields, diffusivity, depth_levels)
    state, height = pl.pallas_call(
        functools.partial(compute_kernel, n_lon, n_lat),
        name="diffuse",
        out_shape=(
            jax.ShapeDtypeStruct(fields.shape, f32),
            jax.ShapeDtypeStruct((lon_cells, lat_cells), f32),
        ),
        in_specs=[hbm] * 5 + [vmem] + [hbm] * 2 + [anywhere] * 5,
        out_specs=(anywhere, vmem),
        scratch_shapes=[
            pltpu.VMEM((lon_cells, lat_cells), f32),
            pltpu.VMEM((lon_cells, lat_cells), f32),
            pltpu.VMEM((lon_cells, lat_cells), jnp.int32),
            pltpu.VMEM((lon_cells, lat_cells), f32),
            pltpu.SMEM((2, levels), f32),
            pltpu.SMEM((2, levels), f32),
            pltpu.VMEM((count, 8, wide), f32),
            pltpu.VMEM((count, 8, wide), f32),
            pltpu.VMEM(fields.shape, f32),
            pltpu.VMEM(halo_shapes[0], f32),
        ]
        + [pltpu.VMEM((tall, wide), f32)] * 6
        + [pltpu.VMEM((count, 8, wide), f32)] * 2
        + [pltpu.VMEM(shape, f32) for shape in halo_shapes[1:]]
        + [
            pltpu.VMEM((PASSES, 8, LANES), f32),
            pltpu.VMEM((2, LANES + 8, LANES), f32),
            pltpu.SemaphoreType.DMA((16,)),
            pltpu.SemaphoreType.DMA((4,)),
        ],
        compiler_params=pltpu.CompilerParams(vmem_limit_bytes=63 * 1024 * 1024),
    )(
        fields, unexplained_elevation, diffusivity, depth_levels, haline_thermal_ratio,
        partners, prior_sigmas, expansion_coefficients, *halos,
    )
    return state.transpose(0, 2, 1, 3), height


def solution(mesh):
    return jax.shard_map(
        functools.partial(local, mesh.shape["lon"], mesh.shape["lat"]),
        mesh=mesh,
        in_specs=(
            P(None, None, "lon", "lat"),
            P("lon", "lat"),
            P("lon", "lat"),
            P("lon", "lat"),
            P(),
            P(),
            P("lon", "lat"),
            P(),
        ),
        out_specs=(P(None, None, "lon", "lat"), P("lon", "lat")),
        check_vma=False,
    )
```
